512 devices in a mesh: snode: 128 (over z, x, core), rhs: 4 (over y).
Axes of the slice: x: 4, y: 4, z: 16, core: 2. Of those that a mesh axis runs over, the one named last changes fastest.
Arguments:
- right_sides: float32 [3, 256, 256, 512], P(None, 'snode', None, 'rhs'), may hold values from -6 to 6
- diag_inverse: float32 [3, 256, 256, 256], P(None, 'snode', 'rhs')
- off_diagonal: bfloat16 [2, 256, 1024, 256], P(None, 'snode'), may hold values from -0.125 to 0.125
- target_snode: int32 [2, 256, 64], P(None, 'snode'), may hold values from 0 to 255, as said below
- target_block: int32 [2, 256, 64], P(None, 'snode'), may hold values from 0 to 15
Outputs:
- solution: float32 [3, 256, 256, 512], P(None, 'snode', None, 'rhs')
The draws below stay inside these ranges and needn't reach their ends.
Inputs may be any that keep to these rules, and one draw needn't show every extreme that they name: `target_snode`: each entry is a supernode's position in the next level; the supernodes at positions i * 2 to i * 2 + 1 belong to index i of snode. Of one level's blocks held by one index of snode, at most 2 name supernodes of any one index, and some index receives exactly 2 from every index in every level.
All inputs are finite; a program needn't handle non-finite values.
Results may differ from the reference program's by a relative error of at most 0.0038.
Values may be sent and summed in bfloat16 or wider, within the bound.
No kernel may reach another device: no remote copies, remote signals or barrier semaphores. Data moves between devices by JAX's collectives and lax.ppermute only.
A program may use at most 64 MiB of HBM per device.

```python
import jax
import jax.numpy as jnp
from jax import lax

W = 256
K = 64
BR = 16
LEVELS = 3
SPL = 2
RHS = 512
NSN = 256
CAP = 2
HOT = 16


def draw_diag_inverse(key, part):
    shape = (LEVELS, NSN, W, W)
    diag_key, noise_key = jax.random.split(key)
    identity = jnp.eye(W, dtype=jnp.float32)
    scales = jnp.exp(jax.random.uniform(diag_key, (LEVELS, NSN, W, 1), jnp.float32, -0.7, 0.4))
    noise = jax.random.normal(noise_key, shape, jnp.float32) * (0.4 / W ** 0.5)
    return identity * scales + noise


def route_level(key):
    owners_count = NSN // SPL
    outgoing = SPL * K
    hot_key, device_key = jax.random.split(key)
    shuffled = jax.random.permutation(hot_key, owners_count).astype(jnp.int32)
    hot_slots = jnp.repeat(shuffled[:HOT], CAP)
    cold_slots = jnp.repeat(shuffled[HOT:], CAP)

    def one_sender(sender):
        pick_key, mix_key, place_key = jax.random.split(jax.random.fold_in(device_key, sender), 3)
        picked = cold_slots[jax.random.permutation(pick_key, cold_slots.shape[0])[:outgoing - HOT * CAP]]
        owners = jnp.concatenate([hot_slots, picked])
        owners = owners[jax.random.permutation(mix_key, outgoing)]
        position = jax.random.randint(place_key, (outgoing,), 0, SPL, jnp.int32)
        return (owners * SPL + position).reshape(SPL, K)
    senders = jnp.arange(owners_count, dtype=jnp.int32)
    return jax.vmap(one_sender)(senders).reshape(NSN, K)


def draw_target_snode(key, part):
    tiers = [route_level(jax.random.fold_in(key, 11 + height)) for height in range(LEVELS - 1)]
    return jnp.stack(tiers, axis=0).astype(jnp.int32)


def place_ends(drawn, key, low, top_value):
    shape = drawn.shape
    place = [jax.random.randint(jax.random.fold_in(key, axis), (), 0, shape[axis]) for axis in range(len(shape))]
    drawn = drawn.at[tuple(place)].set(low)
    longest = shape.index(max(shape))
    place[longest] = (place[longest] + 1) % shape[longest]
    return drawn.at[tuple(place)].set(top_value)


def shard_levels(rng, extent, shards, smallest, high):
    def one(dim, shards_of):
        draws = jax.random.uniform(jax.random.fold_in(jax.random.fold_in(rng, 6), dim), (shards_of,), jnp.float32, smallest / len(shards), high / len(shards))
        return jnp.repeat(jnp.exp(draws), extent[dim] // shards_of).reshape((-1,) + (1,) * (len(extent) - dim - 1))

    factor_of = one(*shards[0])
    for cut in shards[1:]:
        factor_of = factor_of * one(*cut)
    return factor_of


def normal_values(rng, extent, spread, limit, pieces=(), kind=jnp.bfloat16):
    level = shard_levels(rng, extent, pieces, -0.22, 0.18) if pieces else 1.0
    values = jax.random.normal(rng, extent, jnp.float32) * spread * level
    return jnp.minimum(jnp.maximum(values, -limit), limit).astype(kind)


def setup_inputs(seed: int = 0) -> dict:
    keys = jax.random.split(jax.random.key(seed), 6)
    return {
        "right_sides": normal_values(keys[0], (LEVELS, NSN, W, RHS), 1.0, 6.0, ((1, 128), (3, 4)), jnp.float32),
        "diag_inverse": draw_diag_inverse(jax.random.fold_in(keys[5], 71), 0),
        "off_diagonal": normal_values(keys[2], (LEVELS - 1, NSN, K * BR, W), (2 * K * BR) ** -0.5, 0.125, ((1, 128),)),
        "target_snode": draw_target_snode(jax.random.fold_in(keys[5], 71), 0),
        "target_block": place_ends(jax.random.randint(keys[4], (LEVELS - 1, NSN, K), 0, W // BR), jax.random.fold_in(keys[4], 1), 0, (W // BR) - 1).astype(jnp.int32),
    }


def reference(right_sides, diag_inverse, off_diagonal, target_snode, target_block):
    precise = lax.Precision.HIGHEST
    row_blocks = W // BR
    columns = right_sides.shape[3]
    solved = []
    residual = right_sides[0]
    for height in range(LEVELS):
        forward = jnp.einsum("svw,swr->svr", diag_inverse[height], residual, precision=precise)
        solved.append(forward)
        if height + 1 < LEVELS:
            rounded = lax.optimization_barrier(forward.astype(jnp.bfloat16)).astype(jnp.float32)
            update = jnp.einsum("skw,swr->skr", off_diagonal[height].astype(jnp.float32), rounded)
            update = lax.optimization_barrier(update.astype(jnp.bfloat16)).astype(jnp.float32)
            update = update.reshape(NSN * K, BR, columns)
            row_index = (target_snode[height] * row_blocks + target_block[height]).reshape(NSN * K).astype(jnp.int32)
            accumulated = jnp.zeros((NSN * row_blocks, BR, columns), jnp.float32).at[row_index].add(update)
            residual = right_sides[height + 1] - accumulated.reshape(NSN, W, columns)
    answer = [None] * LEVELS
    answer[LEVELS - 1] = jnp.einsum("swv,swr->svr", diag_inverse[LEVELS - 1], solved[LEVELS - 1], precision=precise)
    for height in range(LEVELS - 2, -1, -1):
        above_rows = lax.optimization_barrier(answer[height + 1].astype(jnp.bfloat16)).astype(jnp.float32)
        above_rows = above_rows.reshape(NSN * row_blocks, BR, columns)
        row_index = (target_snode[height] * row_blocks + target_block[height]).reshape(NSN * K).astype(jnp.int32)
        block_rows = above_rows[row_index].reshape(NSN, K * BR, columns)
        carried = solved[height] - jnp.einsum("skw,skr->swr", off_diagonal[height].astype(jnp.float32), block_rows)
        answer[height] = jnp.einsum("swv,swr->svr", diag_inverse[height], carried, precision=precise)
    return jnp.stack(answer, axis=0)
```

```python
import functools

import jax
import jax.numpy as jnp
from jax import lax
from jax.experimental import pallas as pl
from jax.experimental.pallas import tpu as pltpu
from jax.sharding import PartitionSpec as P

BR = 16
F32 = jnp.float32
BF16 = jnp.bfloat16
PRECISE = lax.Precision.HIGHEST


def low_lanes(shape):
    return lax.broadcasted_iota(jnp.int32, shape, len(shape) - 1) < shape[-1] // 2


def swap_lanes(x):
    return pltpu.roll(x, x.shape[-1] // 2, axis=x.ndim - 1)


def doubled(x):
    return jnp.where(low_lanes(x.shape), x, swap_lanes(x))


def pick_half(x, half):
    swapped = swap_lanes(x)
    low = low_lanes(x.shape)
    return jnp.where(low, x, swapped) if half == 0 else jnp.where(low, swapped, x)


def fold(x):
    lanes = x.shape[-1]
    parts = x.reshape(x.shape[0] // BR, 2, BR // 2, lanes)
    top, bottom = parts[:, 0], parts[:, 1]
    return jnp.where(low_lanes(top.shape), top, bottom)


def unfold(x):
    lanes = x.shape[-1]
    blocks = x.reshape(x.shape[0] // (BR // 2), BR // 2, lanes)
    swapped = pltpu.roll(x, lanes // 2, axis=1).reshape(blocks.shape)
    low = low_lanes(blocks.shape)
    top = jnp.where(low, blocks, swapped)
    bottom = jnp.where(low, swapped, blocks)
    return jnp.stack([top, bottom], axis=1).reshape(2 * x.shape[0], lanes)


def whole_diag(diag_ref, s):
    parts = [diag_ref[y, s] for y in range(diag_ref.shape[0])]
    return jnp.concatenate(parts, axis=0)


def solve(diag, x):
    return lax.dot_general(
        diag, x, (((1,), (0,)), ((), ())), precision=PRECISE, preferred_element_type=F32
    )


def solve_transposed(diag, x):
    return lax.dot_general(
        diag, x, (((0,), (0,)), ((), ())), precision=PRECISE, preferred_element_type=F32
    )


def place(table_ref, index_ref, out_ref):
    slots = out_ref.shape[0]

    def body(i, _):
        out_ref[i] = table_ref[index_ref[i]].astype(BF16)
        return 0

    lax.fori_loop(0, slots, body, 0, unroll=8)


def send_updates(nodes, low_ref, off_ref, source_ref, out_ref, table_ref):
    per_node = off_ref.shape[1] // BR
    for s in range(nodes):
        update = jnp.dot(off_ref[s], low_ref[s].astype(BF16), preferred_element_type=F32)
        table_ref[pl.ds(s * per_node, per_node)] = fold(update)
    table_ref[nodes * per_node] = jnp.zeros(table_ref.shape[1:], F32)
    place(table_ref, source_ref, out_ref)


def send_rows(nodes, sol_ref, code_ref, out_ref, table_ref):
    blocks = sol_ref.shape[1] // BR
    for s in range(nodes):
        table_ref[pl.ds(s * blocks, blocks)] = fold(sol_ref[s])
    table_ref[nodes * blocks] = jnp.zeros(table_ref.shape[1:], F32)
    place(table_ref, code_ref, out_ref)


def summed_updates(inbound_ref, gather_ref):
    slots, half_block, lanes = inbound_ref.shape
    rows = inbound_ref[...].astype(F32).reshape(slots * half_block, lanes).astype(BF16)
    return jnp.dot(gather_ref[...], rows, preferred_element_type=F32)


def first_kernel(half, source_ref, diag_ref, rhs_ref, off_ref, low_ref, out_ref, table_ref):
    nodes = rhs_ref.shape[0]
    for s in range(nodes):
        low_ref[s] = solve(whole_diag(diag_ref, s), pick_half(rhs_ref[s], half))
    send_updates(nodes, low_ref, off_ref, source_ref, out_ref, table_ref)


def lower_solve(half, inbound_ref, gather_ref, diag_ref, rhs_ref, low_ref):
    nodes, order, _ = rhs_ref.shape
    total = summed_updates(inbound_ref, gather_ref)
    part = order // 2
    for s in range(nodes):
        residual = pick_half(rhs_ref[s], half) - unfold(total[s * part : (s + 1) * part])
        low_ref[s] = solve(whole_diag(diag_ref, s), residual)


def middle_kernel(
    half, source_ref, inbound_ref, gather_ref, diag_ref, rhs_ref, off_ref, low_ref, out_ref, table_ref
):
    lower_solve(half, inbound_ref, gather_ref, diag_ref, rhs_ref, low_ref)
    send_updates(rhs_ref.shape[0], low_ref, off_ref, source_ref, out_ref, table_ref)


def top_kernel(
    half, code_ref, inbound_ref, gather_ref, diag_ref, rhs_ref, sol_ref, out_ref, low_ref, table_ref
):
    lower_solve(half, inbound_ref, gather_ref, diag_ref, rhs_ref, low_ref)
    nodes = rhs_ref.shape[0]
    for s in range(nodes):
        sol_ref[s] = solve_transposed(whole_diag(diag_ref, s), low_ref[s])
    send_rows(nodes, sol_ref, code_ref, out_ref, table_ref)


def upper_solve(dest_ref, inbound_ref, diag_ref, off_ref, low_ref, sol_ref, rows_ref):
    nodes = off_ref.shape[0]
    per_node = off_ref.shape[1] // BR
    order = off_ref.shape[2]

    def body(k, _):
        rows_ref[k] = inbound_ref[dest_ref[k]].astype(F32)
        return 0

    lax.fori_loop(0, nodes * per_node, body, 0, unroll=8)
    for s in range(nodes):
        blocks = rows_ref[pl.ds(s * per_node, per_node)]
        rows = unfold(blocks.reshape(per_node * BR // 2, blocks.shape[-1])).astype(BF16)
        taken = lax.dot_general(
            off_ref[s], rows, (((0,), (0,)), ((), ())), preferred_element_type=F32
        )
        sol_ref[s] = solve_transposed(whole_diag(diag_ref, s), low_ref[s] - taken)


def upper_kernel(
    dest_ref, code_ref, inbound_ref, diag_ref, off_ref, low_ref, sol_ref, out_ref, rows_ref, table_ref
):
    upper_solve(dest_ref, inbound_ref, diag_ref, off_ref, low_ref, sol_ref, rows_ref)
    send_rows(off_ref.shape[0], sol_ref, code_ref, out_ref, table_ref)


def last_kernel(dest_ref, inbound_ref, diag_ref, off_ref, low_ref, sol_ref, rows_ref):
    upper_solve(dest_ref, inbound_ref, diag_ref, off_ref, low_ref, sol_ref, rows_ref)


def call(kernel, name, scalars, arrays, outs, scratch, flops):
    moved = sum(a.size * a.dtype.itemsize for a in arrays)
    moved += sum(o.size * o.dtype.itemsize for o in outs)
    return pl.pallas_call(
        kernel,
        name=name,
        out_shape=outs,
        in_specs=[pl.BlockSpec(memory_space=pltpu.SMEM)] * len(scalars)
        + [pl.BlockSpec(memory_space=pltpu.VMEM)] * len(arrays),
        out_specs=[pl.BlockSpec(memory_space=pltpu.VMEM)] * len(outs),
        scratch_shapes=scratch,
        compiler_params=pltpu.CompilerParams(vmem_limit_bytes=24 << 20),
        cost_estimate=pl.CostEstimate(flops=flops, bytes_accessed=moved, transcendentals=0),
    )(*scalars, *arrays)


def on_device(right_sides, diag_inverse, off_diagonal, target_snode, target_block):
    levels, nodes, order, lanes = right_sides.shape
    per_node = target_snode.shape[2]
    row_blocks = order // BR
    devices = lax.axis_size("snode")
    outgoing = nodes * per_node
    capacity = 2 * outgoing // devices
    slots = devices * capacity
    local_rows = nodes * row_blocks
    half_block = BR // 2
    halves = range(2)

    block_order = lax.iota(jnp.int32, outgoing)
    slot_ids = lax.iota(jnp.int32, slots)
    sources, destinations, codes = [], [], []
    for h in range(levels - 1):
        flat_target = target_snode[h].reshape(outgoing)
        owner = flat_target // nodes
        row = flat_target % nodes * row_blocks + target_block[h].reshape(outgoing)
        earlier = (owner[:, None] == owner[None, :]) & (block_order[None, :] < block_order[:, None])
        destination = owner * capacity + jnp.sum(earlier.astype(jnp.int32), axis=1)
        placed = destination[None, :] == slot_ids[:, None]
        sources.append(jnp.min(jnp.where(placed, block_order[None, :], outgoing), axis=1))
        codes.append(jnp.min(jnp.where(placed, row[None, :], local_rows), axis=1))
        destinations.append(destination)
    outbound_codes = jnp.stack([c.reshape(devices, capacity) for c in codes], axis=1)
    outbound_codes = outbound_codes.reshape(devices, (levels - 1) * capacity)

    def exchange(x):
        return lax.all_to_all(x, "snode", split_axis=0, concat_axis=0, tiled=True)

    diags = [lax.all_gather(diag_inverse[h], "rhs", axis=0, tiled=False) for h in range(levels)]

    vector = jax.ShapeDtypeStruct((nodes, order, lanes), F32)
    payload = jax.ShapeDtypeStruct((slots, half_block, lanes), BF16)
    update_table = pltpu.VMEM((outgoing + 1, half_block, lanes), F32)
    row_table = pltpu.VMEM((local_rows + 1, half_block, lanes), F32)
    low_scratch = pltpu.VMEM((nodes, order, lanes), F32)
    rows_scratch = pltpu.VMEM((outgoing, half_block, lanes), F32)
    flops = 40 * nodes * order * order * lanes

    lower = [[None] * levels for _ in halves]
    answer = [[None] * levels for _ in halves]
    inbound = [None, None]
    for c in halves:
        lower[c][0], out = call(
            functools.partial(first_kernel, c),
            "first",
            [sources[0]],
            [diags[0], right_sides[0], off_diagonal[0]],
            [vector, payload],
            [update_table],
            flops,
        )
        inbound[c] = exchange(out)

    arrived = exchange(outbound_codes).reshape(devices, levels - 1, capacity)
    arrived = [arrived[:, h].reshape(slots) for h in range(levels - 1)]
    gathers = []
    for h in range(levels - 1):
        wanted = (arrived[h][:, None] * half_block + lax.iota(jnp.int32, half_block)[None, :]).reshape(
            slots * half_block
        )
        rows = lax.iota(jnp.int32, local_rows * half_block)
        gathers.append((rows[:, None] == wanted[None, :]).astype(BF16))

    for h in range(1, levels - 1):
        for c in halves:
            lower[c][h], out = call(
                functools.partial(middle_kernel, c),
                "middle",
                [sources[h]],
                [inbound[c], gathers[h - 1], diags[h], right_sides[h], off_diagonal[h]],
                [vector, payload],
                [update_table],
                flops,
            )
            inbound[c] = exchange(out)
    top = levels - 1
    for c in halves:
        answer[c][top], out = call(
            functools.partial(top_kernel, c),
            "top",
            [arrived[top - 1]],
            [inbound[c], gathers[top - 1], diags[top], right_sides[top]],
            [vector, payload],
            [low_scratch, row_table],
            flops,
        )
        inbound[c] = exchange(out)
    for h in range(levels - 2, 0, -1):
        for c in halves:
            answer[c][h], out = call(
                upper_kernel,
                "upper",
                [destinations[h], arrived[h - 1]],
                [inbound[c], diags[h], off_diagonal[h], lower[c][h]],
                [vector, payload],
                [rows_scratch, row_table],
                flops,
            )
            inbound[c] = exchange(out)
    for c in halves:
        (answer[c][0],) = call(
            last_kernel,
            "last",
            [destinations[0]],
            [inbound[c], diags[0], off_diagonal[0], lower[c][0]],
            [vector],
            [rows_scratch],
            flops,
        )
    low = lax.broadcasted_iota(jnp.int32, (nodes, order, lanes), 2) < lanes // 2
    return jnp.stack([jnp.where(low, answer[0][h], answer[1][h]) for h in range(levels)], axis=0)


def solution(mesh):
    in_specs = (
        P(None, "snode", None, "rhs"),
        P(None, "snode", "rhs", None),
        P(None, "snode", None, None),
        P(None, "snode", None),
        P(None, "snode", None),
    )
    out_specs = P(None, "snode", None, "rhs")
    return jax.shard_map(
        on_device, mesh=mesh, in_specs=in_specs, out_specs=out_specs, check_vma=False
    )
```

```python
import functools

import jax
import jax.numpy as jnp
from jax import lax
from jax.experimental import pallas as pl
from jax.experimental.pallas import tpu as pltpu
from jax.sharding import PartitionSpec as P

BR = 16
HALF = BR // 2
F32 = jnp.float32
BF16 = jnp.bfloat16
PRECISE = lax.Precision.HIGHEST


def whole_diag(diag_ref, s):
    parts = [diag_ref[y, s] for y in range(diag_ref.shape[0])]
    return jnp.concatenate(parts, axis=0)


def solve(diag, x):
    return lax.dot_general(
        diag, x, (((1,), (0,)), ((), ())), precision=PRECISE, preferred_element_type=F32
    )


def solve_transposed(diag, x):
    return lax.dot_general(
        diag, x, (((0,), (0,)), ((), ())), precision=PRECISE, preferred_element_type=F32
    )


def place(table_ref, index_ref, out_ref):
    def body(i, _):
        out_ref[i] = table_ref[index_ref[i]]
        return 0

    lax.fori_loop(0, out_ref.shape[0], body, 0, unroll=8)


def send_updates(low_ref, off_ref, source_ref, out_ref, table_ref):
    nodes, rows, _ = off_ref.shape
    lanes = low_ref.shape[2]
    per_node = rows // BR
    for s in range(nodes):
        update = jnp.dot(off_ref[s], low_ref[s].astype(BF16), preferred_element_type=F32)
        table_ref[pl.ds(s * per_node, per_node)] = update.astype(BF16).reshape(per_node, BR, lanes)
    table_ref[nodes * per_node] = jnp.zeros((BR, lanes), BF16)
    place(table_ref, source_ref, out_ref)


def send_rows(solved, code_ref, out_ref, table_ref):
    blocks, _, lanes = table_ref.shape
    per_node = (blocks - 1) // len(solved)
    for s, values in enumerate(solved):
        table_ref[pl.ds(s * per_node, per_node)] = values.astype(BF16).reshape(per_node, BR, lanes)
    table_ref[blocks - 1] = jnp.zeros((BR, lanes), BF16)
    place(table_ref, code_ref, out_ref)


def summed_updates(inbound_ref, gather_ref):
    slots, _, lanes = inbound_ref.shape
    blocks = inbound_ref[...].astype(F32).reshape(slots, 2, HALF, lanes)
    sums = []
    for part in range(2):
        rows = blocks[:, part].reshape(slots * HALF, lanes).astype(BF16)
        sums.append(jnp.dot(gather_ref[...], rows, preferred_element_type=F32))
    return sums


def lower_solve(inbound_ref, gather_ref, diag_ref, rhs_ref, get_rhs):
    nodes, order, lanes = rhs_ref.shape
    sums = summed_updates(inbound_ref, gather_ref)
    get_rhs.wait()
    part = order // 2
    solved = []
    for s in range(nodes):
        pieces = [x[s * part : (s + 1) * part].reshape(order // BR, HALF, lanes) for x in sums]
        total = jnp.stack(pieces, axis=1).reshape(order, lanes)
        solved.append(solve(whole_diag(diag_ref, s), rhs_ref[s] - total))
    return solved


def fetch(h, pairs, sems):
    copies = [
        pltpu.make_async_copy(array.at[h], buffer, sems.at[i])
        for i, (array, buffer) in enumerate(pairs)
    ]
    for copy in copies:
        copy.start()
    return copies


def store_in_place(h, sol_ref, answer_ref, sem):
    copy = pltpu.make_async_copy(sol_ref, answer_ref.at[h], sem)
    copy.start()
    return copy


def first_kernel(
    source_ref, diag_ref, rhs_hbm, off_hbm, low_ref, out_ref, rhs_ref, off_ref, table_ref, sems
):
    get_rhs, get_off = fetch(0, [(rhs_hbm, rhs_ref), (off_hbm, off_ref)], sems)
    get_rhs.wait()
    for s in range(rhs_ref.shape[0]):
        low_ref[s] = solve(whole_diag(diag_ref, s), rhs_ref[s])
    get_off.wait()
    send_updates(low_ref, off_ref, source_ref, out_ref, table_ref)


def middle_kernel(
    h,
    source_ref,
    inbound_ref,
    gather_ref,
    diag_ref,
    rhs_hbm,
    off_hbm,
    low_ref,
    out_ref,
    rhs_ref,
    off_ref,
    table_ref,
    sems,
):
    get_rhs, get_off = fetch(h, [(rhs_hbm, rhs_ref), (off_hbm, off_ref)], sems)
    for s, solved in enumerate(lower_solve(inbound_ref, gather_ref, diag_ref, rhs_ref, get_rhs)):
        low_ref[s] = solved
    get_off.wait()
    send_updates(low_ref, off_ref, source_ref, out_ref, table_ref)


def top_kernel(
    h,
    code_ref,
    inbound_ref,
    gather_ref,
    diag_ref,
    rhs_hbm,
    answer_ref,
    out_ref,
    rhs_ref,
    sol_ref,
    table_ref,
    sems,
):
    (get_rhs,) = fetch(h, [(rhs_hbm, rhs_ref)], sems)
    solved = lower_solve(inbound_ref, gather_ref, diag_ref, rhs_ref, get_rhs)
    for s, lower in enumerate(solved):
        solved[s] = solve_transposed(whole_diag(diag_ref, s), lower)
        sol_ref[s] = solved[s]
    stored = store_in_place(h, sol_ref, answer_ref, sems.at[1])
    send_rows(solved, code_ref, out_ref, table_ref)
    stored.wait()


def upper_solve(
    dest_ref, inbound_ref, diag_ref, off_ref, low_ref, sol_ref, rows_ref, get_off
):
    nodes, rows, _ = off_ref.shape
    per_node = rows // BR
    lanes = low_ref.shape[2]

    def body(k, _):
        rows_ref[k] = inbound_ref[dest_ref[k]]
        return 0

    lax.fori_loop(0, nodes * per_node, body, 0, unroll=8)
    get_off.wait()
    solved = []
    for s in range(nodes):
        block_rows = rows_ref[pl.ds(s * per_node, per_node)].reshape(rows, lanes)
        taken = lax.dot_general(
            off_ref[s], block_rows, (((0,), (0,)), ((), ())), preferred_element_type=F32
        )
        solved.append(solve_transposed(whole_diag(diag_ref, s), low_ref[s] - taken))
        sol_ref[s] = solved[s]
    return solved


def upper_kernel(
    h,
    dest_ref,
    code_ref,
    inbound_ref,
    diag_ref,
    off_hbm,
    low_ref,
    _,
    answer_ref,
    out_ref,
    off_ref,
    sol_ref,
    rows_ref,
    table_ref,
    sems,
):
    (get_off,) = fetch(h, [(off_hbm, off_ref)], sems)
    solved = upper_solve(
        dest_ref, inbound_ref, diag_ref, off_ref, low_ref, sol_ref, rows_ref, get_off
    )
    stored = store_in_place(h, sol_ref, answer_ref, sems.at[1])
    send_rows(solved, code_ref, out_ref, table_ref)
    stored.wait()


def last_kernel(
    dest_ref, inbound_ref, diag_ref, off_hbm, low_ref, _, answer_ref, off_ref, sol_ref, rows_ref, sems
):
    (get_off,) = fetch(0, [(off_hbm, off_ref)], sems)
    upper_solve(dest_ref, inbound_ref, diag_ref, off_ref, low_ref, sol_ref, rows_ref, get_off)
    store_in_place(0, sol_ref, answer_ref, sems.at[1]).wait()


def scalar(x):
    return x, pl.BlockSpec(memory_space=pltpu.SMEM)


def whole(x):
    return x, pl.BlockSpec(memory_space=pltpu.VMEM)


def in_place(x):
    return x, pl.BlockSpec(memory_space=pl.ANY)


def call(kernel, name, operands, outs, scratch, flops, aliases={}):
    arrays = [x for x, _ in operands]
    moved = sum(x.size * x.dtype.itemsize for x, _ in operands + outs)
    return pl.pallas_call(
        kernel,
        name=name,
        out_shape=[jax.ShapeDtypeStruct(x.shape, x.dtype) for x, _ in outs],
        in_specs=[spec for _, spec in operands],
        out_specs=[spec for _, spec in outs],
        scratch_shapes=scratch,
        input_output_aliases=aliases,
        compiler_params=pltpu.CompilerParams(vmem_limit_bytes=24 << 20),
        cost_estimate=pl.CostEstimate(flops=flops, bytes_accessed=moved, transcendentals=0),
    )(*arrays)


def on_device(right_sides, diag_inverse, off_diagonal, target_snode, target_block):
    levels, nodes, order, lanes = right_sides.shape
    per_node = target_snode.shape[2]
    row_blocks = order // BR
    devices = lax.axis_size("snode")
    outgoing = nodes * per_node
    capacity = 2 * outgoing // devices
    slots = devices * capacity
    local_rows = nodes * row_blocks
    me = lax.axis_index("snode")

    diags = [lax.all_gather(diag_inverse[h], "rhs", axis=0, tiled=False) for h in range(levels)]

    block_order = lax.iota(jnp.int32, outgoing)
    slot_ids = lax.iota(jnp.int32, slots)
    sources, destinations, sent = [], [], []
    for h in range(levels - 1):
        flat_target = target_snode[h].reshape(outgoing)
        owner = flat_target // nodes
        row = flat_target % nodes * row_blocks + target_block[h].reshape(outgoing)
        earlier = (owner[:, None] == owner[None, :]) & (block_order[None, :] < block_order[:, None])
        destination = owner * capacity + jnp.sum(earlier.astype(jnp.int32), axis=1)
        placed = destination[None, :] == slot_ids[:, None]
        sources.append(jnp.min(jnp.where(placed, block_order[None, :], outgoing), axis=1))
        destinations.append(destination)
        sent.append(destination * local_rows + row)

    def exchange(x):
        return lax.all_to_all(x, "snode", split_axis=0, concat_axis=0, tiled=True)

    vector = jax.ShapeDtypeStruct((nodes, order, lanes), F32)
    payload = whole(jax.ShapeDtypeStruct((slots, BR, lanes), BF16))
    table = pltpu.VMEM((outgoing + 1, BR, lanes), BF16)
    row_table = pltpu.VMEM((local_rows + 1, BR, lanes), BF16)
    rows_scratch = pltpu.VMEM((outgoing, BR, lanes), BF16)
    flops = 40 * nodes * order * order * lanes

    rhs_buffer = pltpu.VMEM(vector.shape, F32)
    off_buffer = pltpu.VMEM(off_diagonal.shape[1:], BF16)
    sems = pltpu.SemaphoreType.DMA((2,))

    lower = [None] * (levels - 1)
    lower[0], out = call(
        first_kernel,
        "first",
        [scalar(sources[0]), whole(diags[0]), in_place(right_sides), in_place(off_diagonal)],
        [whole(vector), payload],
        [rhs_buffer, off_buffer, table, sems],
        flops,
    )
    inbound = exchange(out)

    everyone = lax.all_gather(jnp.stack(sent), "snode", axis=0, tiled=False)
    arrived, gathers = [], []
    for h in range(levels - 1):
        slot = everyone[:, h] // local_rows
        row = everyone[:, h] % local_rows
        found = [
            jnp.min(jnp.where(slot == me * capacity + i, row, local_rows), axis=1)
            for i in range(capacity)
        ]
        code = jnp.stack(found, axis=1).reshape(slots)
        arrived.append(code)
        wanted = (code[:, None] * HALF + lax.iota(jnp.int32, HALF)[None, :]).reshape(slots * HALF)
        rows = lax.iota(jnp.int32, local_rows * HALF)
        gathers.append((rows[:, None] == wanted[None, :]).astype(BF16))

    for h in range(1, levels - 1):
        lower[h], out = call(
            functools.partial(middle_kernel, h),
            "middle",
            [scalar(sources[h]), whole(inbound), whole(gathers[h - 1]), whole(diags[h])]
            + [in_place(right_sides), in_place(off_diagonal)],
            [whole(vector), payload],
            [rhs_buffer, off_buffer, table, sems],
            flops,
        )
        inbound = exchange(out)
    top = levels - 1
    answer = jax.ShapeDtypeStruct(right_sides.shape, F32)
    answer, out = call(
        functools.partial(top_kernel, top),
        "top",
        [scalar(arrived[top - 1]), whole(inbound), whole(gathers[top - 1]), whole(diags[top])]
        + [in_place(right_sides)],
        [in_place(answer), payload],
        [rhs_buffer, rhs_buffer, row_table, sems],
        flops,
    )
    inbound = exchange(out)
    for h in range(levels - 2, 0, -1):
        answer, out = call(
            functools.partial(upper_kernel, h),
            "upper",
            [scalar(destinations[h]), scalar(arrived[h - 1]), whole(inbound), whole(diags[h])]
            + [in_place(off_diagonal), whole(lower[h]), in_place(answer)],
            [in_place(answer), payload],
            [off_buffer, rhs_buffer, rows_scratch, row_table, sems],
            flops,
            {6: 0},
        )
        inbound = exchange(out)
    (answer,) = call(
        last_kernel,
        "last",
        [scalar(destinations[0]), whole(inbound), whole(diags[0])]
        + [in_place(off_diagonal), whole(lower[0]), in_place(answer)],
        [in_place(answer)],
        [off_buffer, rhs_buffer, rows_scratch, sems],
        flops,
        {5: 0},
    )
    return answer


def solution(mesh):
    in_specs = (
        P(None, "snode", None, "rhs"),
        P(None, "snode", "rhs", None),
        P(None, "snode", None, None),
        P(None, "snode", None),
        P(None, "snode", None),
    )
    out_specs = P(None, "snode", None, "rhs")
    return jax.shard_map(
        on_device, mesh=mesh, in_specs=in_specs, out_specs=out_specs, check_vma=False
    )
```

```python
import functools

import jax
import jax.numpy as jnp
from jax import lax
from jax.experimental import pallas as pl
from jax.experimental.pallas import tpu as pltpu
from jax.sharding import PartitionSpec as P

BR = 16
HALF = BR // 2
F32 = jnp.float32
BF16 = jnp.bfloat16
PRECISE = lax.Precision.HIGHEST


def whole_diag(diag_ref, s):
    parts = [diag_ref[y, s] for y in range(diag_ref.shape[0])]
    return jnp.concatenate(parts, axis=0)


def solve(diag, x):
    return lax.dot_general(
        diag, x, (((1,), (0,)), ((), ())), precision=PRECISE, preferred_element_type=F32
    )


def solve_transposed(diag, x):
    return lax.dot_general(
        diag, x, (((0,), (0,)), ((), ())), precision=PRECISE, preferred_element_type=F32
    )


def place(table_ref, index_ref, staged_ref, out_ref, sems):
    chunks = sems.shape[0]
    size = out_ref.shape[0] // chunks
    copies = []
    for c in range(chunks):

        def body(i, _):
            staged_ref[i] = table_ref[index_ref[i]]
            return 0

        lax.fori_loop(c * size, (c + 1) * size, body, 0, unroll=8)
        part = pl.ds(c * size, size)
        copies.append(pltpu.make_async_copy(staged_ref.at[part], out_ref.at[part], sems.at[c]))
        copies[-1].start()
    return copies


def send_updates(low_ref, off_ref, source_ref, staged_ref, out_ref, table_ref, sems):
    nodes, rows, _ = off_ref.shape
    lanes = low_ref.shape[2]
    per_node = rows // BR
    for s in range(nodes):
        update = jnp.dot(off_ref[s], low_ref[s].astype(BF16), preferred_element_type=F32)
        table_ref[pl.ds(s * per_node, per_node)] = update.astype(BF16).reshape(per_node, BR, lanes)
    table_ref[nodes * per_node] = jnp.zeros((BR, lanes), BF16)
    return place(table_ref, source_ref, staged_ref, out_ref, sems)


def send_rows(solved, code_ref, staged_ref, out_ref, table_ref, sems):
    blocks, _, lanes = table_ref.shape
    per_node = (blocks - 1) // len(solved)
    for s, values in enumerate(solved):
        table_ref[pl.ds(s * per_node, per_node)] = values.astype(BF16).reshape(per_node, BR, lanes)
    table_ref[blocks - 1] = jnp.zeros((BR, lanes), BF16)
    return place(table_ref, code_ref, staged_ref, out_ref, sems)


def fetch(pairs, sems):
    copies = [pltpu.make_async_copy(a, b, sems.at[i]) for i, (a, b) in enumerate(pairs)]
    for copy in copies:
        copy.start()
    return copies


def store(source, target, sem):
    copy = pltpu.make_async_copy(source, target, sem)
    copy.start()
    return copy


def finish(copies):
    for copy in copies:
        copy.wait()


def summed_updates(inbound_ref, gather_ref):
    slots, _, lanes = inbound_ref.shape
    blocks = inbound_ref[...].astype(F32).reshape(slots, 2, HALF, lanes)
    sums = []
    for part in range(2):
        rows = blocks[:, part].reshape(slots * HALF, lanes).astype(BF16)
        sums.append(jnp.dot(gather_ref[...], rows, preferred_element_type=F32))
    return sums


def lower_solve(inbound_ref, gather_ref, diag_ref, rhs_ref, get_gather, get_others):
    nodes, order, lanes = rhs_ref.shape
    get_gather.wait()
    sums = summed_updates(inbound_ref, gather_ref)
    finish(get_others)
    part = order // 2
    solved = []
    for s in range(nodes):
        pieces = [x[s * part : (s + 1) * part].reshape(order // BR, HALF, lanes) for x in sums]
        total = jnp.stack(pieces, axis=1).reshape(order, lanes)
        solved.append(solve(whole_diag(diag_ref, s), rhs_ref[s] - total))
    return solved


def first_kernel(
    source_ref,
    diag_hbm,
    rhs_hbm,
    off_hbm,
    low_hbm,
    out_hbm,
    diag_ref,
    rhs_ref,
    off_ref,
    low_ref,
    table_ref,
    staged_ref,
    in_sems,
    low_sem,
    out_sems,
):
    pairs = [(diag_hbm, diag_ref), (rhs_hbm.at[0], rhs_ref), (off_hbm.at[0], off_ref)]
    get_diag, get_rhs, get_off = fetch(pairs, in_sems)
    finish([get_diag, get_rhs])
    for s in range(rhs_ref.shape[0]):
        low_ref[s] = solve(whole_diag(diag_ref, s), rhs_ref[s])
    kept = store(low_ref, low_hbm, low_sem.at[0])
    get_off.wait()
    finish(send_updates(low_ref, off_ref, source_ref, staged_ref, out_hbm, table_ref, out_sems))
    kept.wait()


def middle_kernel(
    h,
    source_ref,
    inbound_ref,
    gather_hbm,
    diag_hbm,
    rhs_hbm,
    off_hbm,
    low_hbm,
    out_hbm,
    gather_ref,
    diag_ref,
    rhs_ref,
    off_ref,
    low_ref,
    table_ref,
    staged_ref,
    in_sems,
    low_sem,
    out_sems,
):
    pairs = [(gather_hbm, gather_ref), (diag_hbm, diag_ref)]
    pairs += [(rhs_hbm.at[h], rhs_ref), (off_hbm.at[h], off_ref)]
    get_gather, get_diag, get_rhs, get_off = fetch(pairs, in_sems)
    solved = lower_solve(inbound_ref, gather_ref, diag_ref, rhs_ref, get_gather, [get_diag, get_rhs])
    for s, values in enumerate(solved):
        low_ref[s] = values
    kept = store(low_ref, low_hbm, low_sem.at[0])
    get_off.wait()
    finish(send_updates(low_ref, off_ref, source_ref, staged_ref, out_hbm, table_ref, out_sems))
    kept.wait()


def top_kernel(
    h,
    code_ref,
    inbound_ref,
    gather_hbm,
    diag_hbm,
    rhs_hbm,
    answer_hbm,
    out_hbm,
    gather_ref,
    diag_ref,
    rhs_ref,
    sol_ref,
    table_ref,
    staged_ref,
    in_sems,
    sol_sem,
    out_sems,
):
    pairs = [(gather_hbm, gather_ref), (diag_hbm, diag_ref), (rhs_hbm.at[h], rhs_ref)]
    get_gather, get_diag, get_rhs = fetch(pairs, in_sems)
    solved = lower_solve(inbound_ref, gather_ref, diag_ref, rhs_ref, get_gather, [get_diag, get_rhs])
    for s, lower in enumerate(solved):
        solved[s] = solve_transposed(whole_diag(diag_ref, s), lower)
        sol_ref[s] = solved[s]
    kept = store(sol_ref, answer_hbm.at[h], sol_sem.at[0])
    finish(send_rows(solved, code_ref, staged_ref, out_hbm, table_ref, out_sems))
    kept.wait()


def upper_solve(
    h, dest_ref, inbound_ref, diag_hbm, off_hbm, low_hbm, diag_ref, off_ref, low_ref, sol_ref, rows_ref, sems
):
    pairs = [(off_hbm.at[h], off_ref), (diag_hbm, diag_ref), (low_hbm, low_ref)]
    copies = fetch(pairs, sems)
    nodes, rows, _ = off_ref.shape
    per_node = rows // BR
    lanes = low_ref.shape[2]

    def body(k, _):
        rows_ref[k] = inbound_ref[dest_ref[k]]
        return 0

    lax.fori_loop(0, nodes * per_node, body, 0, unroll=8)
    finish(copies)
    solved = []
    for s in range(nodes):
        block_rows = rows_ref[pl.ds(s * per_node, per_node)].reshape(rows, lanes)
        taken = lax.dot_general(
            off_ref[s], block_rows, (((0,), (0,)), ((), ())), preferred_element_type=F32
        )
        solved.append(solve_transposed(whole_diag(diag_ref, s), low_ref[s] - taken))
        sol_ref[s] = solved[s]
    return solved


def upper_kernel(
    h,
    dest_ref,
    code_ref,
    inbound_ref,
    diag_hbm,
    off_hbm,
    low_hbm,
    _,
    answer_hbm,
    out_hbm,
    diag_ref,
    off_ref,
    low_ref,
    sol_ref,
    rows_ref,
    table_ref,
    staged_ref,
    in_sems,
    sol_sem,
    out_sems,
):
    solved = upper_solve(
        h, dest_ref, inbound_ref, diag_hbm, off_hbm, low_hbm,
        diag_ref, off_ref, low_ref, sol_ref, rows_ref, in_sems,
    )
    kept = store(sol_ref, answer_hbm.at[h], sol_sem.at[0])
    finish(send_rows(solved, code_ref, staged_ref, out_hbm, table_ref, out_sems))
    kept.wait()


def last_kernel(
    dest_ref,
    inbound_ref,
    diag_hbm,
    off_hbm,
    low_hbm,
    _,
    answer_hbm,
    diag_ref,
    off_ref,
    low_ref,
    sol_ref,
    rows_ref,
    in_sems,
    sol_sem,
):
    upper_solve(
        0, dest_ref, inbound_ref, diag_hbm, off_hbm, low_hbm,
        diag_ref, off_ref, low_ref, sol_ref, rows_ref, in_sems,
    )
    store(sol_ref, answer_hbm.at[0], sol_sem.at[0]).wait()


def scalar(x):
    return x, pl.BlockSpec(memory_space=pltpu.SMEM)


def whole(x):
    return x, pl.BlockSpec(memory_space=pltpu.VMEM)


def far(x):
    return x, pl.BlockSpec(memory_space=pltpu.HBM)


def call(kernel, name, operands, outs, scratch, flops, aliases={}):
    arrays = [x for x, _ in operands]
    moved = sum(x.size * x.dtype.itemsize for x, _ in operands + outs)
    return pl.pallas_call(
        kernel,
        name=name,
        out_shape=[jax.ShapeDtypeStruct(x.shape, x.dtype) for x, _ in outs],
        in_specs=[spec for _, spec in operands],
        out_specs=[spec for _, spec in outs],
        scratch_shapes=scratch,
        input_output_aliases=aliases,
        cost_estimate=pl.CostEstimate(flops=flops, bytes_accessed=moved, transcendentals=0),
    )(*arrays)


def ring_groups(devices, inner=8):
    if devices % inner:
        return [[list(range(devices))]]
    near = [list(range(start, start + inner)) for start in range(0, devices, inner)]
    return [near, [list(column) for column in zip(*near)]]


def on_device(right_sides, diag_inverse, off_diagonal, target_snode, target_block):
    levels, nodes, order, lanes = right_sides.shape
    per_node = target_snode.shape[2]
    row_blocks = order // BR
    devices = lax.axis_size("snode")
    outgoing = nodes * per_node
    capacity = 2 * outgoing // devices
    slots = devices * capacity
    local_rows = nodes * row_blocks
    me = lax.axis_index("snode")

    diags = [lax.all_gather(diag_inverse[h], "rhs", axis=0, tiled=False) for h in range(levels)]

    block_order = lax.iota(jnp.int32, outgoing)
    slot_ids = lax.iota(jnp.int32, slots)
    sources, destinations, sent = [], [], []
    for h in range(levels - 1):
        flat_target = target_snode[h].reshape(outgoing)
        owner = flat_target // nodes
        row = flat_target % nodes * row_blocks + target_block[h].reshape(outgoing)
        earlier = (owner[:, None] == owner[None, :]) & (block_order[None, :] < block_order[:, None])
        destination = owner * capacity + jnp.sum(earlier.astype(jnp.int32), axis=1)
        placed = destination[None, :] == slot_ids[:, None]
        sources.append(jnp.min(jnp.where(placed, block_order[None, :], outgoing), axis=1))
        destinations.append(destination)
        sent.append(destination * local_rows + row)

    def exchange(x):
        return lax.all_to_all(x, "snode", split_axis=0, concat_axis=0, tiled=True)

    vector = far(jax.ShapeDtypeStruct((nodes, order, lanes), F32))
    payload = far(jax.ShapeDtypeStruct((slots, BR, lanes), BF16))
    answer = jax.ShapeDtypeStruct(right_sides.shape, F32)
    one = pltpu.SemaphoreType.DMA((1,))
    inputs = pltpu.SemaphoreType.DMA((4,))
    vectors = pltpu.VMEM((nodes, order, lanes), F32)
    off_buffer = pltpu.VMEM(off_diagonal.shape[1:], BF16)
    diag_buffer = pltpu.VMEM(diags[0].shape, F32)
    gather_buffer = pltpu.VMEM((local_rows * HALF, slots * HALF), BF16)
    table = pltpu.VMEM((outgoing + 1, BR, lanes), BF16)
    row_table = pltpu.VMEM((local_rows + 1, BR, lanes), BF16)
    rows_scratch = pltpu.VMEM((outgoing, BR, lanes), BF16)
    send = [pltpu.VMEM((slots, BR, lanes), BF16), inputs, one, pltpu.SemaphoreType.DMA((4,))]
    flops = 40 * nodes * order * order * lanes

    lower = [None] * (levels - 1)
    lower[0], out = call(
        first_kernel,
        "first",
        [scalar(sources[0]), far(diags[0]), far(right_sides), far(off_diagonal)],
        [vector, payload],
        [diag_buffer, vectors, off_buffer, vectors, table] + send,
        flops,
    )
    inbound = exchange(out)

    everyone = jnp.stack(sent)
    for groups in ring_groups(devices):
        everyone = lax.all_gather(everyone, "snode", axis_index_groups=groups, axis=0, tiled=False)
    everyone = everyone.reshape(devices, levels - 1, outgoing)
    arrived, gathers = [], []
    for h in range(levels - 1):
        slot = everyone[:, h] // local_rows
        row = everyone[:, h] % local_rows
        found = [
            jnp.min(jnp.where(slot == me * capacity + i, row, local_rows), axis=1)
            for i in range(capacity)
        ]
        code = jnp.stack(found, axis=1).reshape(slots)
        arrived.append(code)
        wanted = (code[:, None] * HALF + lax.iota(jnp.int32, HALF)[None, :]).reshape(slots * HALF)
        rows = lax.iota(jnp.int32, local_rows * HALF)
        gathers.append((rows[:, None] == wanted[None, :]).astype(BF16))

    for h in range(1, levels - 1):
        lower[h], out = call(
            functools.partial(middle_kernel, h),
            "middle",
            [scalar(sources[h]), whole(inbound), far(gathers[h - 1]), far(diags[h])]
            + [far(right_sides), far(off_diagonal)],
            [vector, payload],
            [gather_buffer, diag_buffer, vectors, off_buffer, vectors, table] + send,
            flops,
        )
        inbound = exchange(out)
    top = levels - 1
    answer, out = call(
        functools.partial(top_kernel, top),
        "top",
        [scalar(arrived[top - 1]), whole(inbound), far(gathers[top - 1]), far(diags[top])]
        + [far(right_sides)],
        [far(answer), payload],
        [gather_buffer, diag_buffer, vectors, vectors, row_table] + send,
        flops,
    )
    inbound = exchange(out)
    for h in range(levels - 2, 0, -1):
        answer, out = call(
            functools.partial(upper_kernel, h),
            "upper",
            [scalar(destinations[h]), scalar(arrived[h - 1]), whole(inbound), far(diags[h])]
            + [far(off_diagonal), far(lower[h]), far(answer)],
            [far(answer), payload],
            [diag_buffer, off_buffer, vectors, vectors, rows_scratch, row_table] + send,
            flops,
            {6: 0},
        )
        inbound = exchange(out)
    (answer,) = call(
        last_kernel,
        "last",
        [scalar(destinations[0]), whole(inbound), far(diags[0])]
        + [far(off_diagonal), far(lower[0]), far(answer)],
        [far(answer)],
        [diag_buffer, off_buffer, vectors, vectors, rows_scratch, inputs, one],
        flops,
        {5: 0},
    )
    return answer


def solution(mesh):
    in_specs = (
        P(None, "snode", None, "rhs"),
        P(None, "snode", "rhs", None),
        P(None, "snode", None, None),
        P(None, "snode", None),
        P(None, "snode", None),
    )
    out_specs = P(None, "snode", None, "rhs")
    return jax.shard_map(
        on_device, mesh=mesh, in_specs=in_specs, out_specs=out_specs, check_vma=False
    )
```

```python
import functools

import jax
import jax.numpy as jnp
from jax import lax
from jax.experimental import pallas as pl
from jax.experimental.pallas import tpu as pltpu
from jax.sharding import PartitionSpec as P

BR = 16
HALF = BR // 2
F32 = jnp.float32
BF16 = jnp.bfloat16
PRECISE = lax.Precision.HIGHEST


def whole_diag(diag_ref, s):
    parts = [diag_ref[y, s] for y in range(diag_ref.shape[0])]
    return jnp.concatenate(parts, axis=0)


def solve(diag, x):
    return lax.dot_general(
        diag, x, (((1,), (0,)), ((), ())), precision=PRECISE, preferred_element_type=F32
    )


def solve_transposed(diag, x):
    return lax.dot_general(
        diag, x, (((0,), (0,)), ((), ())), precision=PRECISE, preferred_element_type=F32
    )


def place(table_ref, index_ref, staged_ref, out_ref, sems):
    chunks = sems.shape[0]
    size = out_ref.shape[0] // chunks
    copies = []
    for c in range(chunks):

        def body(i, _):
            staged_ref[i] = table_ref[index_ref[i]]
            return 0

        lax.fori_loop(c * size, (c + 1) * size, body, 0, unroll=8)
        part = pl.ds(c * size, size)
        copies.append(pltpu.make_async_copy(staged_ref.at[part], out_ref.at[part], sems.at[c]))
        copies[-1].start()
    return copies


def send_updates(low_ref, off_ref, source_ref, staged_ref, out_ref, table_ref, sems):
    nodes, rows, _ = off_ref.shape
    lanes = low_ref.shape[2]
    per_node = rows // BR
    for s in range(nodes):
        update = jnp.dot(off_ref[s], low_ref[s].astype(BF16), preferred_element_type=F32)
        table_ref[pl.ds(s * per_node, per_node)] = update.astype(BF16).reshape(per_node, BR, lanes)
    table_ref[nodes * per_node] = jnp.zeros((BR, lanes), BF16)
    return place(table_ref, source_ref, staged_ref, out_ref, sems)


def fill_rows(solved, table_ref):
    blocks, _, lanes = table_ref.shape
    per_node = (blocks - 1) // len(solved)
    for s, values in enumerate(solved):
        table_ref[pl.ds(s * per_node, per_node)] = values.astype(BF16).reshape(per_node, BR, lanes)
    table_ref[blocks - 1] = jnp.zeros((BR, lanes), BF16)


def send_rows(solved, code_ref, staged_ref, out_ref, table_ref, sems):
    fill_rows(solved, table_ref)
    return place(table_ref, code_ref, staged_ref, out_ref, sems)


def place_rows(solved, code_ref, out_ref, table_ref):
    fill_rows(solved, table_ref)

    def body(i, _):
        out_ref[i] = table_ref[code_ref[i]]
        return 0

    lax.fori_loop(0, out_ref.shape[0], body, 0, unroll=8)


def fetch(pairs, sems):
    copies = [pltpu.make_async_copy(a, b, sems.at[i]) for i, (a, b) in enumerate(pairs)]
    for copy in copies:
        copy.start()
    return copies


def store(source, target, sem):
    copy = pltpu.make_async_copy(source, target, sem)
    copy.start()
    return copy


def finish(copies):
    for copy in copies:
        copy.wait()


def partial_sums(inbound_ref, gather_ref, part, size):
    lanes = inbound_ref.shape[2]
    blocks = inbound_ref[pl.ds(part * size, size)].astype(F32).reshape(size, 2, HALF, lanes)
    chosen = gather_ref[:, part * size * HALF : (part + 1) * size * HALF]
    sums = []
    for half in range(2):
        rows = blocks[:, half].reshape(size * HALF, lanes).astype(BF16)
        sums.append(jnp.dot(chosen, rows, preferred_element_type=F32))
    return sums


def diag_copies(place_ref, own_hbm, part_hbms, diag_ref):
    sources = [own_hbm] + list(part_hbms)
    return [(source, diag_ref.at[place_ref[i]]) for i, source in enumerate(sources)]


def lower_solve(inbound_hbm, inbound_ref, gather_hbm, gather_ref, diag_ref, rhs_ref, others, sems):
    nodes, order, lanes = rhs_ref.shape
    chunks = 4
    size = inbound_ref.shape[0] // chunks
    pairs = [(gather_hbm, gather_ref)]
    for c in range(chunks):
        part = pl.ds(c * size, size)
        pairs.append((inbound_hbm.at[part], inbound_ref.at[part]))
    copies = fetch(pairs + others, sems)
    copies[0].wait()
    sums = None
    for c in range(chunks):
        copies[1 + c].wait()
        found = partial_sums(inbound_ref, gather_ref, c, size)
        sums = found if sums is None else [x + y for x, y in zip(sums, found)]
    rest = copies[1 + chunks :]
    finish(rest[:NEEDED])
    part = order // 2
    solved = []
    for s in range(nodes):
        pieces = [x[s * part : (s + 1) * part].reshape(order // BR, HALF, lanes) for x in sums]
        total = jnp.stack(pieces, axis=1).reshape(order, lanes)
        solved.append(solve(whole_diag(diag_ref, s), rhs_ref[s] - total))
    return solved, rest[NEEDED:]


NEEDED = 5


def first_kernel(
    source_ref,
    place_ref,
    diag_hbm,
    part1_hbm,
    part2_hbm,
    part3_hbm,
    rhs_hbm,
    off_hbm,
    low_hbm,
    whole_hbm,
    out_hbm,
    diag_ref,
    rhs_ref,
    off_ref,
    low_ref,
    table_ref,
    staged_ref,
    in_sems,
    keep_sems,
    out_sems,
):
    pairs = diag_copies(place_ref, diag_hbm.at[0], [part1_hbm, part2_hbm, part3_hbm], diag_ref)
    pairs += [(rhs_hbm.at[0], rhs_ref), (off_hbm.at[0], off_ref)]
    copies = fetch(pairs, in_sems)
    finish(copies[:NEEDED])
    kept = [store(diag_ref, whole_hbm, keep_sems.at[0])]
    for s in range(rhs_ref.shape[0]):
        low_ref[s] = solve(whole_diag(diag_ref, s), rhs_ref[s])
    kept.append(store(low_ref, low_hbm, keep_sems.at[1]))
    finish(copies[NEEDED:])
    kept += send_updates(low_ref, off_ref, source_ref, staged_ref, out_hbm, table_ref, out_sems)
    finish(kept)


def middle_kernel(
    h,
    source_ref,
    place_ref,
    inbound_hbm,
    gather_hbm,
    diag_hbm,
    part1_hbm,
    part2_hbm,
    part3_hbm,
    rhs_hbm,
    off_hbm,
    low_hbm,
    whole_hbm,
    out_hbm,
    inbound_ref,
    gather_ref,
    diag_ref,
    rhs_ref,
    off_ref,
    low_ref,
    table_ref,
    staged_ref,
    in_sems,
    keep_sems,
    out_sems,
):
    pairs = diag_copies(place_ref, diag_hbm.at[h], [part1_hbm, part2_hbm, part3_hbm], diag_ref)
    pairs += [(rhs_hbm.at[h], rhs_ref), (off_hbm.at[h], off_ref)]
    solved, late = lower_solve(
        inbound_hbm, inbound_ref, gather_hbm, gather_ref, diag_ref, rhs_ref, pairs, in_sems
    )
    kept = [store(diag_ref, whole_hbm, keep_sems.at[0])]
    for s, values in enumerate(solved):
        low_ref[s] = values
    kept.append(store(low_ref, low_hbm, keep_sems.at[1]))
    finish(late)
    kept += send_updates(low_ref, off_ref, source_ref, staged_ref, out_hbm, table_ref, out_sems)
    finish(kept)


def top_kernel(
    h,
    code_ref,
    place_ref,
    inbound_hbm,
    gather_hbm,
    diag_hbm,
    part1_hbm,
    part2_hbm,
    part3_hbm,
    rhs_hbm,
    answer_hbm,
    out_hbm,
    inbound_ref,
    gather_ref,
    diag_ref,
    rhs_ref,
    sol_ref,
    table_ref,
    staged_ref,
    in_sems,
    keep_sems,
    out_sems,
):
    pairs = diag_copies(place_ref, diag_hbm.at[h], [part1_hbm, part2_hbm, part3_hbm], diag_ref)
    pairs += [(rhs_hbm.at[h], rhs_ref)]
    solved, _ = lower_solve(
        inbound_hbm, inbound_ref, gather_hbm, gather_ref, diag_ref, rhs_ref, pairs, in_sems
    )
    for s, lower in enumerate(solved):
        solved[s] = solve_transposed(whole_diag(diag_ref, s), lower)
        sol_ref[s] = solved[s]
    kept = [store(sol_ref, answer_hbm.at[h], keep_sems.at[0])]
    kept += send_rows(solved, code_ref, staged_ref, out_hbm, table_ref, out_sems)
    finish(kept)


def upper_solve(h, dest_ref, inbound_ref, diag_ref, off_hbm, low_ref, off_ref, sol_ref, rows_ref, sem):
    (get_off,) = fetch([(off_hbm.at[h], off_ref)], sem)
    nodes, rows, _ = off_ref.shape
    per_node = rows // BR
    lanes = low_ref.shape[2]

    def body(k, _):
        rows_ref[k] = inbound_ref[dest_ref[k]]
        return 0

    lax.fori_loop(0, nodes * per_node, body, 0, unroll=8)
    get_off.wait()
    solved = []
    for s in range(nodes):
        block_rows = rows_ref[pl.ds(s * per_node, per_node)].reshape(rows, lanes)
        taken = lax.dot_general(
            off_ref[s], block_rows, (((0,), (0,)), ((), ())), preferred_element_type=F32
        )
        solved.append(solve_transposed(whole_diag(diag_ref, s), low_ref[s] - taken))
        sol_ref[s] = solved[s]
    return solved


def upper_kernel(
    h,
    dest_ref,
    code_ref,
    inbound_ref,
    diag_ref,
    off_hbm,
    low_ref,
    _,
    answer_hbm,
    out_ref,
    off_ref,
    sol_ref,
    rows_ref,
    table_ref,
    sems,
):
    solved = upper_solve(
        h, dest_ref, inbound_ref, diag_ref, off_hbm, low_ref, off_ref, sol_ref, rows_ref, sems
    )
    kept = store(sol_ref, answer_hbm.at[h], sems.at[1])
    place_rows(solved, code_ref, out_ref, table_ref)
    kept.wait()


def last_kernel(
    dest_ref, inbound_ref, diag_ref, off_hbm, low_ref, _, answer_hbm, off_ref, sol_ref, rows_ref, sems
):
    upper_solve(
        0, dest_ref, inbound_ref, diag_ref, off_hbm, low_ref, off_ref, sol_ref, rows_ref, sems
    )
    store(sol_ref, answer_hbm.at[0], sems.at[1]).wait()


def scalar(x):
    return x, pl.BlockSpec(memory_space=pltpu.SMEM)


def whole(x):
    return x, pl.BlockSpec(memory_space=pltpu.VMEM)


def far(x):
    return x, pl.BlockSpec(memory_space=pltpu.HBM)


def anywhere(x):
    return x, pl.BlockSpec(memory_space=pl.ANY)


def call(kernel, name, operands, outs, scratch, flops, aliases={}, limit=None):
    arrays = [x for x, _ in operands]
    moved = sum(x.size * x.dtype.itemsize for x, _ in operands + outs)
    return pl.pallas_call(
        kernel,
        name=name,
        out_shape=[jax.ShapeDtypeStruct(x.shape, x.dtype) for x, _ in outs],
        in_specs=[spec for _, spec in operands],
        out_specs=[spec for _, spec in outs],
        scratch_shapes=scratch,
        input_output_aliases=aliases,
        compiler_params=pltpu.CompilerParams(vmem_limit_bytes=limit),
        cost_estimate=pl.CostEstimate(flops=flops, bytes_accessed=moved, transcendentals=0),
    )(*arrays)


def on_device(right_sides, diag_inverse, off_diagonal, target_snode, target_block):
    levels, nodes, order, lanes = right_sides.shape
    per_node = target_snode.shape[2]
    row_blocks = order // BR
    devices = lax.axis_size("snode")
    sharers = lax.axis_size("rhs")
    outgoing = nodes * per_node
    capacity = 2 * outgoing // devices
    slots = devices * capacity
    local_rows = nodes * row_blocks
    couplings = levels - 1

    def diag_parts(h):
        mine = diag_inverse[h]
        steps = [[(y, (y + k) % sharers) for y in range(sharers)] for k in range(1, sharers)]
        return [lax.ppermute(mine, "rhs", step) for step in steps]

    mine = lax.axis_index("rhs")
    places = (mine - lax.iota(jnp.int32, sharers)) % sharers

    parts = [diag_parts(0)]

    block_order = lax.iota(jnp.int32, outgoing)
    flat_target = target_snode.reshape(couplings, outgoing)
    owner = flat_target // nodes
    row = flat_target % nodes * row_blocks + target_block.reshape(couplings, outgoing)
    earlier = (owner[:, :, None] == owner[:, None, :]) & (
        block_order[None, None, :] < block_order[None, :, None]
    )
    destinations = owner * capacity + jnp.sum(earlier.astype(jnp.int32), axis=2)
    slot_ids = lax.iota(jnp.int32, slots)
    placed = destinations[:, None, :] == slot_ids[None, :, None]
    sources = jnp.min(jnp.where(placed, block_order[None, None, :], outgoing), axis=2)
    ids = slot_ids.reshape(devices, 1, capacity, 1)
    placed = destinations[None, :, None, :] == ids
    sent = jnp.min(jnp.where(placed, row[None, :, None, :], local_rows), axis=3)

    def exchange(x):
        return lax.all_to_all(x, "snode", split_axis=0, concat_axis=0, tiled=True)

    arrived = exchange(sent.reshape(devices, couplings * capacity))

    vector = far(jax.ShapeDtypeStruct((nodes, order, lanes), F32))
    payload = far(jax.ShapeDtypeStruct((slots, BR, lanes), BF16))
    near_payload = whole(payload[0])
    gathered = far(jax.ShapeDtypeStruct((sharers,) + diag_inverse.shape[1:], F32))
    answer = jax.ShapeDtypeStruct(right_sides.shape, F32)
    two = pltpu.SemaphoreType.DMA((2,))
    inputs = pltpu.SemaphoreType.DMA((12,))
    vectors = pltpu.VMEM((nodes, order, lanes), F32)
    off_buffer = pltpu.VMEM(off_diagonal.shape[1:], BF16)
    diag_buffer = pltpu.VMEM(gathered[0].shape, F32)
    gather_buffer = pltpu.VMEM((local_rows * HALF, slots * HALF), BF16)
    table = pltpu.VMEM((outgoing + 1, BR, lanes), BF16)
    row_table = pltpu.VMEM((local_rows + 1, BR, lanes), BF16)
    rows_scratch = pltpu.VMEM((outgoing, BR, lanes), BF16)
    blocks_buffer = pltpu.VMEM((slots, BR, lanes), BF16)
    send = [blocks_buffer, inputs, two, pltpu.SemaphoreType.DMA((4,))]
    flops = 40 * nodes * order * order * lanes
    small = 24 << 20

    def diag_operands(h):
        return [far(diag_inverse)] + [far(x) for x in parts[h]]

    lower, whole_diags = [None] * couplings, [None] * couplings
    lower[0], whole_diags[0], out = call(
        first_kernel,
        "first",
        [scalar(sources[0]), scalar(places)]
        + diag_operands(0)
        + [far(right_sides), far(off_diagonal)],
        [vector, gathered, payload],
        [diag_buffer, vectors, off_buffer, vectors, table] + send,
        flops,
    )
    inbound = exchange(out)

    codes, gathers = [], []
    for h in range(couplings):
        code = arrived[:, h * capacity : (h + 1) * capacity].reshape(slots)
        codes.append(code)
        wanted = (code[:, None] * HALF + lax.iota(jnp.int32, HALF)[None, :]).reshape(slots * HALF)
        rows = lax.iota(jnp.int32, local_rows * HALF)
        gathers.append((rows[:, None] == wanted[None, :]).astype(BF16))

    for h in range(1, couplings):
        parts.append(diag_parts(h))
        lower[h], whole_diags[h], out = call(
            functools.partial(middle_kernel, h),
            "middle",
            [scalar(sources[h]), scalar(places), far(inbound), far(gathers[h - 1])]
            + diag_operands(h)
            + [far(right_sides), far(off_diagonal)],
            [vector, gathered, payload],
            [blocks_buffer, gather_buffer, diag_buffer, vectors, off_buffer, vectors, table] + send,
            flops,
        )
        inbound = exchange(out)
    top = couplings
    parts.append(diag_parts(top))
    answer, out = call(
        functools.partial(top_kernel, top),
        "top",
        [scalar(codes[top - 1]), scalar(places), far(inbound), far(gathers[top - 1])]
        + diag_operands(top)
        + [far(right_sides)],
        [far(answer), payload],
        [blocks_buffer, gather_buffer, diag_buffer, vectors, vectors, row_table] + send,
        flops,
    )
    inbound = exchange(out)
    for h in range(couplings - 1, 0, -1):
        answer, out = call(
            functools.partial(upper_kernel, h),
            "upper",
            [scalar(destinations[h]), scalar(codes[h - 1]), whole(inbound), whole(whole_diags[h])]
            + [anywhere(off_diagonal), whole(lower[h]), anywhere(answer)],
            [anywhere(answer), near_payload],
            [off_buffer, vectors, rows_scratch, row_table, two],
            flops,
            {6: 0},
            small,
        )
        inbound = exchange(out)
    (answer,) = call(
        last_kernel,
        "last",
        [scalar(destinations[0]), whole(inbound), whole(whole_diags[0])]
        + [anywhere(off_diagonal), whole(lower[0]), anywhere(answer)],
        [anywhere(answer)],
        [off_buffer, vectors, rows_scratch, two],
        flops,
        {5: 0},
        small,
    )
    return answer


def solution(mesh):
    in_specs = (
        P(None, "snode", None, "rhs"),
        P(None, "snode", "rhs", None),
        P(None, "snode", None, None),
        P(None, "snode", None),
        P(None, "snode", None),
    )
    out_specs = P(None, "snode", None, "rhs")
    return jax.shard_map(
        on_device, mesh=mesh, in_specs=in_specs, out_specs=out_specs, check_vma=False
    )
```

```python
import functools

import jax
import jax.numpy as jnp
from jax import lax
from jax.experimental import pallas as pl
from jax.experimental.pallas import tpu as pltpu
from jax.sharding import PartitionSpec as P

BR = 16
CAPACITY = 2
F32 = jnp.float32
BF16 = jnp.bfloat16
PRECISE = lax.Precision.HIGHEST


def whole_diag(diag_ref, s):
    parts = [diag_ref[y, s] for y in range(diag_ref.shape[0])]
    return jnp.concatenate(parts, axis=0)


def solve(diag, x):
    return lax.dot_general(
        diag, x, (((1,), (0,)), ((), ())), precision=PRECISE, preferred_element_type=F32
    )


def solve_transposed(diag, x):
    return lax.dot_general(
        diag, x, (((0,), (0,)), ((), ())), precision=PRECISE, preferred_element_type=F32
    )


def place(table_ref, index, capacity, staged_ref, out_ref, sems):
    chunks = sems.shape[0]
    peers = out_ref.shape[0] // capacity // chunks
    copies = []
    for c in range(chunks):
        place_chunk(table_ref, index, capacity, staged_ref, c * peers, peers)
        part = pl.ds(c * peers * capacity, peers * capacity)
        copies.append(pltpu.make_async_copy(staged_ref.at[part], out_ref.at[part], sems.at[c]))
        copies[-1].start()
    return copies


def place_chunk(table_ref, index, capacity, out_ref, start, peers):
    def body(d, _):
        for i in range(capacity):
            out_ref[d * capacity + i] = table_ref[index(d, i)]
        return 0

    lax.fori_loop(start, start + peers, body, 0, unroll=4)


def source_index(h, capacity, source_ref):
    return lambda d, i: source_ref[h, d * capacity + i]


def code_index(h, capacity, code_ref):
    return lambda d, i: code_ref[h * capacity + i, d]


def send_updates(h, low_ref, off_ref, source_ref, staged_ref, out_ref, table_ref, sems):
    nodes, rows, _ = off_ref.shape
    lanes = low_ref.shape[2]
    per_node = rows // BR
    for s in range(nodes):
        update = jnp.dot(off_ref[s], low_ref[s].astype(BF16), preferred_element_type=F32)
        table_ref[pl.ds(s * per_node, per_node)] = update.astype(BF16).reshape(per_node, BR, lanes)
    table_ref[nodes * per_node] = jnp.zeros((BR, lanes), BF16)
    index = source_index(h, CAPACITY, source_ref)
    return place(table_ref, index, CAPACITY, staged_ref, out_ref, sems)


def fill_rows(solved, table_ref):
    blocks, _, lanes = table_ref.shape
    per_node = (blocks - 1) // len(solved)
    for s, values in enumerate(solved):
        table_ref[pl.ds(s * per_node, per_node)] = values.astype(BF16).reshape(per_node, BR, lanes)
    table_ref[blocks - 1] = jnp.zeros((BR, lanes), BF16)


def send_rows(h, solved, code_ref, staged_ref, out_ref, table_ref, sems):
    fill_rows(solved, table_ref)
    index = code_index(h, CAPACITY, code_ref)
    return place(table_ref, index, CAPACITY, staged_ref, out_ref, sems)


def place_rows(h, solved, code_ref, out_ref, table_ref):
    fill_rows(solved, table_ref)
    index = code_index(h, CAPACITY, code_ref)
    place_chunk(table_ref, index, CAPACITY, out_ref, 0, out_ref.shape[0] // CAPACITY)


def fetch(pairs, sems):
    copies = [pltpu.make_async_copy(a, b, sems.at[i]) for i, (a, b) in enumerate(pairs)]
    for copy in copies:
        copy.start()
    return copies


def store(source, target, sem):
    copy = pltpu.make_async_copy(source, target, sem)
    copy.start()
    return copy


def finish(copies):
    for copy in copies:
        copy.wait()


def add_blocks(inbound_ref, index, sum_refs, start, peers):
    step = len(sum_refs) // CAPACITY

    def body(g, _):
        for e in range(step):
            d = g * step + e
            for i in range(CAPACITY):
                sum_ref = sum_refs[e * CAPACITY + i]
                code = index(d, i)
                sum_ref[code] = sum_ref[code] + inbound_ref[d * CAPACITY + i].astype(F32)
        return 0

    lax.fori_loop(start // step, (start + peers) // step, body, 0, unroll=2)


def diag_copies(place_ref, own_hbm, part_hbms, diag_ref):
    sources = [own_hbm] + list(part_hbms)
    return [(source, diag_ref.at[place_ref[i]]) for i, source in enumerate(sources)]


def lower_solve(inbound_hbm, inbound_ref, index, sum_refs, diag_ref, rhs_ref, others, sems):
    nodes, order, lanes = rhs_ref.shape
    chunks = 4
    size = inbound_ref.shape[0] // chunks
    pairs = []
    for c in range(chunks):
        part = pl.ds(c * size, size)
        pairs.append((inbound_hbm.at[part], inbound_ref.at[part]))
    copies = fetch(pairs + others, sems)
    for sum_ref in sum_refs:
        sum_ref[...] = jnp.zeros_like(sum_ref)
    for c in range(chunks):
        copies[c].wait()
        add_blocks(inbound_ref, index, sum_refs, c * size // CAPACITY, size // CAPACITY)
    rest = copies[chunks:]
    finish(rest[:NEEDED])
    blocks = order // BR
    solved = []
    for s in range(nodes):
        part = pl.ds(s * blocks, blocks)
        total = sum(sum_ref[part] for sum_ref in sum_refs).reshape(order, lanes)
        solved.append(solve(whole_diag(diag_ref, s), rhs_ref[s] - total))
    return solved, rest[NEEDED:]


NEEDED = 5


def first_kernel(
    source_ref,
    place_ref,
    diag_hbm,
    part1_hbm,
    part2_hbm,
    part3_hbm,
    rhs_hbm,
    off_hbm,
    low_hbm,
    whole_hbm,
    out_hbm,
    diag_ref,
    rhs_ref,
    off_ref,
    low_ref,
    table_ref,
    staged_ref,
    in_sems,
    keep_sems,
    out_sems,
):
    pairs = diag_copies(place_ref, diag_hbm.at[0], [part1_hbm, part2_hbm, part3_hbm], diag_ref)
    pairs += [(rhs_hbm.at[0], rhs_ref), (off_hbm.at[0], off_ref)]
    copies = fetch(pairs, in_sems)
    finish(copies[:NEEDED])
    kept = [store(diag_ref, whole_hbm, keep_sems.at[0])]
    for s in range(rhs_ref.shape[0]):
        low_ref[s] = solve(whole_diag(diag_ref, s), rhs_ref[s])
    kept.append(store(low_ref, low_hbm, keep_sems.at[1]))
    finish(copies[NEEDED:])
    kept += send_updates(0, low_ref, off_ref, source_ref, staged_ref, out_hbm, table_ref, out_sems)
    finish(kept)


def middle_kernel(
    h,
    source_ref,
    place_ref,
    code_ref,
    inbound_hbm,
    diag_hbm,
    part1_hbm,
    part2_hbm,
    part3_hbm,
    rhs_hbm,
    off_hbm,
    low_hbm,
    whole_hbm,
    out_hbm,
    sum0_ref,
    sum1_ref,
    sum2_ref,
    sum3_ref,
    inbound_ref,
    diag_ref,
    rhs_ref,
    off_ref,
    low_ref,
    table_ref,
    staged_ref,
    in_sems,
    keep_sems,
    out_sems,
):
    pairs = diag_copies(place_ref, diag_hbm.at[h], [part1_hbm, part2_hbm, part3_hbm], diag_ref)
    pairs += [(rhs_hbm.at[h], rhs_ref), (off_hbm.at[h], off_ref)]
    sums = [sum0_ref, sum1_ref, sum2_ref, sum3_ref]
    index = code_index(h - 1, CAPACITY, code_ref)
    solved, late = lower_solve(
        inbound_hbm, inbound_ref, index, sums, diag_ref, rhs_ref, pairs, in_sems
    )
    kept = [store(diag_ref, whole_hbm, keep_sems.at[0])]
    for s, values in enumerate(solved):
        low_ref[s] = values
    kept.append(store(low_ref, low_hbm, keep_sems.at[1]))
    finish(late)
    kept += send_updates(h, low_ref, off_ref, source_ref, staged_ref, out_hbm, table_ref, out_sems)
    finish(kept)


def top_kernel(
    h,
    place_ref,
    code_ref,
    inbound_hbm,
    diag_hbm,
    part1_hbm,
    part2_hbm,
    part3_hbm,
    rhs_hbm,
    answer_hbm,
    out_hbm,
    sum0_ref,
    sum1_ref,
    sum2_ref,
    sum3_ref,
    inbound_ref,
    diag_ref,
    rhs_ref,
    sol_ref,
    table_ref,
    staged_ref,
    in_sems,
    keep_sems,
    out_sems,
):
    pairs = diag_copies(place_ref, diag_hbm.at[h], [part1_hbm, part2_hbm, part3_hbm], diag_ref)
    pairs += [(rhs_hbm.at[h], rhs_ref)]
    sums = [sum0_ref, sum1_ref, sum2_ref, sum3_ref]
    index = code_index(h - 1, CAPACITY, code_ref)
    solved, _ = lower_solve(
        inbound_hbm, inbound_ref, index, sums, diag_ref, rhs_ref, pairs, in_sems
    )
    for s, lower in enumerate(solved):
        solved[s] = solve_transposed(whole_diag(diag_ref, s), lower)
        sol_ref[s] = solved[s]
    kept = [store(sol_ref, answer_hbm.at[h], keep_sems.at[0])]
    kept += send_rows(h - 1, solved, code_ref, staged_ref, out_hbm, table_ref, out_sems)
    finish(kept)


def upper_solve(
    h, dest_ref, inbound_ref, diag_hbm, off_hbm, low_hbm, diag_ref, off_ref, low_ref, sol_ref, rows_ref, sems
):
    pairs = [(off_hbm.at[h], off_ref), (low_hbm, low_ref), (diag_hbm, diag_ref)]
    get_off, get_low, get_diag = fetch(pairs, sems)
    nodes, rows, _ = off_ref.shape
    per_node = rows // BR
    lanes = low_ref.shape[2]

    def body(k, _):
        rows_ref[k] = inbound_ref[dest_ref[h, k]]
        return 0

    lax.fori_loop(0, nodes * per_node, body, 0, unroll=8)
    get_off.wait()
    taken = []
    for s in range(nodes):
        block_rows = rows_ref[pl.ds(s * per_node, per_node)].reshape(rows, lanes)
        taken.append(
            lax.dot_general(
                off_ref[s], block_rows, (((0,), (0,)), ((), ())), preferred_element_type=F32
            )
        )
    finish([get_low, get_diag])
    solved = []
    for s in range(nodes):
        solved.append(solve_transposed(whole_diag(diag_ref, s), low_ref[s] - taken[s]))
        sol_ref[s] = solved[s]
    return solved


def upper_kernel(
    h,
    dest_ref,
    code_ref,
    inbound_ref,
    diag_hbm,
    off_hbm,
    low_hbm,
    _,
    answer_hbm,
    out_ref,
    diag_ref,
    off_ref,
    low_ref,
    sol_ref,
    rows_ref,
    table_ref,
    sems,
):
    solved = upper_solve(
        h, dest_ref, inbound_ref, diag_hbm, off_hbm, low_hbm,
        diag_ref, off_ref, low_ref, sol_ref, rows_ref, sems,
    )
    kept = store(sol_ref, answer_hbm.at[h], sems.at[3])
    place_rows(h - 1, solved, code_ref, out_ref, table_ref)
    kept.wait()


def last_kernel(
    dest_ref,
    inbound_ref,
    diag_hbm,
    off_hbm,
    low_hbm,
    _,
    answer_hbm,
    diag_ref,
    off_ref,
    low_ref,
    sol_ref,
    rows_ref,
    sems,
):
    upper_solve(
        0, dest_ref, inbound_ref, diag_hbm, off_hbm, low_hbm,
        diag_ref, off_ref, low_ref, sol_ref, rows_ref, sems,
    )
    store(sol_ref, answer_hbm.at[0], sems.at[3]).wait()


def scalar(x):
    return x, pl.BlockSpec(memory_space=pltpu.SMEM)


def whole(x):
    return x, pl.BlockSpec(memory_space=pltpu.VMEM)


def far(x):
    return x, pl.BlockSpec(memory_space=pltpu.HBM)


def anywhere(x):
    return x, pl.BlockSpec(memory_space=pl.ANY)


def call(kernel, name, operands, outs, scratch, flops, aliases={}, limit=None):
    arrays = [x for x, _ in operands]
    moved = sum(x.size * x.dtype.itemsize for x, _ in operands + outs)
    return pl.pallas_call(
        kernel,
        name=name,
        out_shape=[jax.ShapeDtypeStruct(x.shape, x.dtype) for x, _ in outs],
        in_specs=[spec for _, spec in operands],
        out_specs=[spec for _, spec in outs],
        scratch_shapes=scratch,
        input_output_aliases=aliases,
        compiler_params=pltpu.CompilerParams(vmem_limit_bytes=limit),
        cost_estimate=pl.CostEstimate(flops=flops, bytes_accessed=moved, transcendentals=0),
    )(*arrays)


def on_device(right_sides, diag_inverse, off_diagonal, target_snode, target_block):
    levels, nodes, order, lanes = right_sides.shape
    per_node = target_snode.shape[2]
    row_blocks = order // BR
    devices = lax.axis_size("snode")
    sharers = lax.axis_size("rhs")
    outgoing = nodes * per_node
    capacity = CAPACITY
    slots = devices * capacity
    local_rows = nodes * row_blocks
    couplings = levels - 1

    def diag_parts(mine):
        steps = [[(y, (y + k) % sharers) for y in range(sharers)] for k in range(1, sharers)]
        return [lax.ppermute(mine, "rhs", step) for step in steps]

    mine = lax.axis_index("rhs")
    places = (mine - lax.iota(jnp.int32, sharers)) % sharers

    parts = [diag_parts(diag_inverse[0])]

    block_order = lax.iota(jnp.int32, outgoing)
    flat_target = target_snode.reshape(couplings, outgoing)
    owner = flat_target // nodes
    row = flat_target % nodes * row_blocks + target_block.reshape(couplings, outgoing)
    earlier = (owner[:, :, None] == owner[:, None, :]) & (
        block_order[None, None, :] < block_order[None, :, None]
    )
    destinations = owner * capacity + jnp.sum(earlier.astype(jnp.int32), axis=2)
    slot_ids = lax.iota(jnp.int32, slots)
    placed = destinations[:, None, :] == slot_ids[None, :, None]
    sources = jnp.min(jnp.where(placed, block_order[None, None, :], outgoing), axis=2)
    ids = slot_ids.reshape(devices, 1, capacity, 1)
    placed = destinations[None, :, None, :] == ids
    sent = jnp.min(jnp.where(placed, row[None, :, None, :], local_rows), axis=3)

    def exchange(x):
        return lax.all_to_all(x, "snode", split_axis=0, concat_axis=0, tiled=True)

    vector = far(jax.ShapeDtypeStruct((nodes, order, lanes), F32))
    payload = far(jax.ShapeDtypeStruct((slots, BR, lanes), BF16))
    near_payload = whole(payload[0])
    gathered = far(jax.ShapeDtypeStruct((sharers,) + diag_inverse.shape[1:], F32))
    answer = jax.ShapeDtypeStruct(right_sides.shape, F32)
    four = pltpu.SemaphoreType.DMA((4,))
    two = pltpu.SemaphoreType.DMA((2,))
    inputs = pltpu.SemaphoreType.DMA((12,))
    vectors = pltpu.VMEM((nodes, order, lanes), F32)
    off_buffer = pltpu.VMEM(off_diagonal.shape[1:], BF16)
    diag_buffer = pltpu.VMEM(gathered[0].shape, F32)
    sums = [pltpu.VMEM((local_rows + 1, BR, lanes), F32)] * 4
    table = pltpu.VMEM((outgoing + 1, BR, lanes), BF16)
    row_table = pltpu.VMEM((local_rows + 1, BR, lanes), BF16)
    rows_scratch = pltpu.VMEM((outgoing, BR, lanes), BF16)
    blocks_buffer = pltpu.VMEM((slots, BR, lanes), BF16)
    send = [blocks_buffer, inputs, two, pltpu.SemaphoreType.DMA((4,))]
    flops = 40 * nodes * order * order * lanes
    small = 24 << 20

    def diag_operands(h):
        return [far(diag_inverse)] + [far(x) for x in parts[h]]

    lower, whole_diags = [None] * couplings, [None] * couplings
    lower[0], whole_diags[0], out = call(
        first_kernel,
        "first",
        [scalar(sources), scalar(places)]
        + diag_operands(0)
        + [far(right_sides), far(off_diagonal)],
        [vector, gathered, payload],
        [diag_buffer, vectors, off_buffer, vectors, table] + send,
        flops,
    )
    later_diags, out = lax.optimization_barrier((diag_inverse, out))
    pairs_of_rows = capacity * BR // 2
    carried = sent.reshape(devices, 1, 1, couplings * capacity).astype(BF16)
    carried = jnp.pad(carried, ((0, 0), (0, 0), (0, 1), (0, lanes - couplings * capacity)))
    out = jnp.concatenate([out.reshape(devices, pairs_of_rows, 2, lanes), carried], axis=1)
    inbound = exchange(out)
    codes = inbound[:, pairs_of_rows, 0, : couplings * capacity].astype(jnp.int32).T
    inbound = inbound[:, :pairs_of_rows].reshape(slots, BR, lanes)

    for h in range(1, couplings):
        parts.append(diag_parts(later_diags[h]))
        lower[h], whole_diags[h], out = call(
            functools.partial(middle_kernel, h),
            "middle",
            [scalar(sources), scalar(places), scalar(codes), far(inbound)]
            + diag_operands(h)
            + [far(right_sides), far(off_diagonal)],
            [vector, gathered, payload],
            sums + [blocks_buffer, diag_buffer, vectors, off_buffer, vectors, table] + send,
            flops,
        )
        inbound = exchange(out)
    top = couplings
    parts.append(diag_parts(later_diags[top]))
    answer, out = call(
        functools.partial(top_kernel, top),
        "top",
        [scalar(places), scalar(codes), far(inbound)]
        + diag_operands(top)
        + [far(right_sides)],
        [far(answer), payload],
        sums + [blocks_buffer, diag_buffer, vectors, vectors, row_table] + send,
        flops,
    )
    inbound = exchange(out)
    for h in range(couplings - 1, 0, -1):
        answer, out = call(
            functools.partial(upper_kernel, h),
            "upper",
            [scalar(destinations), scalar(codes), whole(inbound), anywhere(whole_diags[h])]
            + [anywhere(off_diagonal), anywhere(lower[h]), anywhere(answer)],
            [anywhere(answer), near_payload],
            [diag_buffer, off_buffer, vectors, vectors, rows_scratch, row_table, four],
            flops,
            {6: 0},
            small,
        )
        inbound = exchange(out)
    (answer,) = call(
        last_kernel,
        "last",
        [scalar(destinations), whole(inbound), anywhere(whole_diags[0])]
        + [anywhere(off_diagonal), anywhere(lower[0]), anywhere(answer)],
        [anywhere(answer)],
        [diag_buffer, off_buffer, vectors, vectors, rows_scratch, four],
        flops,
        {5: 0},
        small,
    )
    return answer


def solution(mesh):
    in_specs = (
        P(None, "snode", None, "rhs"),
        P(None, "snode", "rhs", None),
        P(None, "snode", None, None),
        P(None, "snode", None),
        P(None, "snode", None),
    )
    out_specs = P(None, "snode", None, "rhs")
    return jax.shard_map(
        on_device, mesh=mesh, in_specs=in_specs, out_specs=out_specs, check_vma=False
    )
```

```python
import functools

import jax
import jax.numpy as jnp
from jax import lax
from jax.experimental import pallas as pl
from jax.experimental.pallas import tpu as pltpu
from jax.sharding import PartitionSpec as P

BR = 16
CAPACITY = 2
F32 = jnp.float32
BF16 = jnp.bfloat16
PRECISE = lax.Precision.HIGHEST


def whole_diag(diag_ref, s):
    parts = [diag_ref[y, s] for y in range(diag_ref.shape[0])]
    return jnp.concatenate(parts, axis=0)


def solve(diag, x):
    return lax.dot_general(
        diag, x, (((1,), (0,)), ((), ())), precision=PRECISE, preferred_element_type=F32
    )


def solve_transposed(diag, x):
    return lax.dot_general(
        diag, x, (((0,), (0,)), ((), ())), precision=PRECISE, preferred_element_type=F32
    )


def place(table_ref, index, capacity, staged_ref, out_ref, sems):
    chunks = sems.shape[0]
    peers = out_ref.shape[0] // capacity // chunks
    copies = []
    for c in range(chunks):
        place_chunk(table_ref, index, capacity, staged_ref, c * peers, peers)
        part = pl.ds(c * peers * capacity, peers * capacity)
        copies.append(pltpu.make_async_copy(staged_ref.at[part], out_ref.at[part], sems.at[c]))
        copies[-1].start()
    return copies


def place_chunk(table_ref, index, capacity, out_ref, start, peers):
    def body(d, _):
        for i in range(capacity):
            out_ref[d * capacity + i] = table_ref[index(d, i)]
        return 0

    lax.fori_loop(start, start + peers, body, 0, unroll=16)


def source_index(h, capacity, source_ref):
    return lambda d, i: source_ref[h, d * capacity + i]


def code_index(h, capacity, code_ref):
    return lambda d, i: code_ref[h * capacity + i, d]


def send_updates(h, low_ref, off_ref, source_ref, staged_ref, out_ref, table_ref, sems):
    nodes, rows, _ = off_ref.shape
    lanes = low_ref.shape[2]
    per_node = rows // BR
    for s in range(nodes):
        update = jnp.dot(off_ref[s], low_ref[s].astype(BF16), preferred_element_type=F32)
        table_ref[pl.ds(s * per_node, per_node)] = update.astype(BF16).reshape(per_node, BR, lanes)
    table_ref[nodes * per_node] = jnp.zeros((BR, lanes), BF16)
    index = source_index(h, CAPACITY, source_ref)
    return place(table_ref, index, CAPACITY, staged_ref, out_ref, sems)


def fill_rows(solved, table_ref):
    blocks, _, lanes = table_ref.shape
    per_node = (blocks - 1) // len(solved)
    for s, values in enumerate(solved):
        table_ref[pl.ds(s * per_node, per_node)] = values.astype(BF16).reshape(per_node, BR, lanes)
    table_ref[blocks - 1] = jnp.zeros((BR, lanes), BF16)


def send_rows(h, solved, code_ref, staged_ref, out_ref, table_ref, sems):
    fill_rows(solved, table_ref)
    index = code_index(h, CAPACITY, code_ref)
    return place(table_ref, index, CAPACITY, staged_ref, out_ref, sems)


def place_rows(h, solved, code_ref, out_ref, table_ref):
    fill_rows(solved, table_ref)
    index = code_index(h, CAPACITY, code_ref)
    place_chunk(table_ref, index, CAPACITY, out_ref, 0, out_ref.shape[0] // CAPACITY)


def fetch(pairs, sems):
    copies = [pltpu.make_async_copy(a, b, sems.at[i]) for i, (a, b) in enumerate(pairs)]
    for copy in copies:
        copy.start()
    return copies


def store(source, target, sem):
    copy = pltpu.make_async_copy(source, target, sem)
    copy.start()
    return copy


def finish(copies):
    for copy in copies:
        copy.wait()


def add_blocks(inbound_ref, index, sum_refs, start, peers):
    step = len(sum_refs) // CAPACITY

    def body(g, _):
        for e in range(step):
            d = g * step + e
            for i in range(CAPACITY):
                sum_ref = sum_refs[e * CAPACITY + i]
                code = index(d, i)
                sum_ref[code] = sum_ref[code] + inbound_ref[d * CAPACITY + i].astype(F32)
        return 0

    lax.fori_loop(start // step, (start + peers) // step, body, 0, unroll=4)


def diag_copies(own_hbm, part_hbms, diag_ref):
    sharers = diag_ref.shape[0]
    mine = lax.axis_index("rhs")
    sources = [own_hbm] + list(part_hbms)
    return [
        (source, diag_ref.at[lax.rem(mine + (sharers - i), sharers)])
        for i, source in enumerate(sources)
    ]


def lower_solve(code_hbm, code_ref, inbound_hbm, inbound_ref, index, sum_refs, diag_ref, rhs_ref, others, sems):
    nodes, order, lanes = rhs_ref.shape
    chunks = 4
    size = inbound_ref.shape[0] // chunks
    pairs = []
    for c in range(chunks):
        part = pl.ds(c * size, size)
        pairs.append((inbound_hbm.at[part], inbound_ref.at[part]))
    copies = fetch([(code_hbm, code_ref)] + pairs + others, sems)
    get_code, copies = copies[0], copies[1:]
    for sum_ref in sum_refs:
        sum_ref[...] = jnp.zeros_like(sum_ref)
    get_code.wait()
    for c in range(chunks):
        copies[c].wait()
        add_blocks(inbound_ref, index, sum_refs, c * size // CAPACITY, size // CAPACITY)
    rest = copies[chunks:]
    finish(rest[:NEEDED])
    blocks = order // BR
    solved = []
    for s in range(nodes):
        part = pl.ds(s * blocks, blocks)
        total = sum(sum_ref[part] for sum_ref in sum_refs).reshape(order, lanes)
        solved.append(solve(whole_diag(diag_ref, s), rhs_ref[s] - total))
    return solved, rest[NEEDED:]


NEEDED = 5


def first_kernel(
    source_hbm,
    diag_hbm,
    part1_hbm,
    part2_hbm,
    part3_hbm,
    rhs_hbm,
    off_hbm,
    low_hbm,
    whole_hbm,
    out_hbm,
    source_ref,
    diag_ref,
    rhs_ref,
    off_ref,
    low_ref,
    table_ref,
    staged_ref,
    in_sems,
    keep_sems,
    out_sems,
):
    pairs = diag_copies(diag_hbm.at[0], [part1_hbm, part2_hbm, part3_hbm], diag_ref)
    pairs += [(rhs_hbm.at[0], rhs_ref), (off_hbm.at[0], off_ref), (source_hbm, source_ref)]
    copies = fetch(pairs, in_sems)
    finish(copies[:NEEDED])
    kept = [store(diag_ref, whole_hbm, keep_sems.at[0])]
    for s in range(rhs_ref.shape[0]):
        low_ref[s] = solve(whole_diag(diag_ref, s), rhs_ref[s])
    kept.append(store(low_ref, low_hbm, keep_sems.at[1]))
    finish(copies[NEEDED:])
    kept += send_updates(0, low_ref, off_ref, source_ref, staged_ref, out_hbm, table_ref, out_sems)
    finish(kept)


def middle_kernel(
    h,
    source_hbm,
    code_hbm,
    inbound_hbm,
    diag_hbm,
    part1_hbm,
    part2_hbm,
    part3_hbm,
    rhs_hbm,
    off_hbm,
    low_hbm,
    whole_hbm,
    out_hbm,
    sum0_ref,
    sum1_ref,
    sum2_ref,
    sum3_ref,
    source_ref,
    code_ref,
    inbound_ref,
    diag_ref,
    rhs_ref,
    off_ref,
    low_ref,
    table_ref,
    staged_ref,
    in_sems,
    keep_sems,
    out_sems,
):
    later = [part_hbm.at[h - 1] for part_hbm in (part1_hbm, part2_hbm, part3_hbm)]
    pairs = diag_copies(diag_hbm.at[h], later, diag_ref)
    pairs += [(rhs_hbm.at[h], rhs_ref), (off_hbm.at[h], off_ref), (source_hbm, source_ref)]
    sums = [sum0_ref, sum1_ref, sum2_ref, sum3_ref]
    index = code_index(h - 1, CAPACITY, code_ref)
    solved, late = lower_solve(
        code_hbm, code_ref, inbound_hbm, inbound_ref, index, sums, diag_ref, rhs_ref, pairs, in_sems
    )
    kept = [store(diag_ref, whole_hbm, keep_sems.at[0])]
    for s, values in enumerate(solved):
        low_ref[s] = values
    kept.append(store(low_ref, low_hbm, keep_sems.at[1]))
    finish(late)
    kept += send_updates(h, low_ref, off_ref, source_ref, staged_ref, out_hbm, table_ref, out_sems)
    finish(kept)


def top_kernel(
    h,
    code_hbm,
    inbound_hbm,
    diag_hbm,
    part1_hbm,
    part2_hbm,
    part3_hbm,
    rhs_hbm,
    answer_hbm,
    out_hbm,
    sum0_ref,
    sum1_ref,
    sum2_ref,
    sum3_ref,
    code_ref,
    inbound_ref,
    diag_ref,
    rhs_ref,
    sol_ref,
    table_ref,
    staged_ref,
    in_sems,
    keep_sems,
    out_sems,
):
    later = [part_hbm.at[h - 1] for part_hbm in (part1_hbm, part2_hbm, part3_hbm)]
    pairs = diag_copies(diag_hbm.at[h], later, diag_ref)
    pairs += [(rhs_hbm.at[h], rhs_ref)]
    sums = [sum0_ref, sum1_ref, sum2_ref, sum3_ref]
    index = code_index(h - 1, CAPACITY, code_ref)
    solved, _ = lower_solve(
        code_hbm, code_ref, inbound_hbm, inbound_ref, index, sums, diag_ref, rhs_ref, pairs, in_sems
    )
    for s, lower in enumerate(solved):
        solved[s] = solve_transposed(whole_diag(diag_ref, s), lower)
        sol_ref[s] = solved[s]
    kept = [store(sol_ref, answer_hbm.at[h], keep_sems.at[0])]
    kept += send_rows(h - 1, solved, code_ref, staged_ref, out_hbm, table_ref, out_sems)
    finish(kept)


def upper_solve(
    h, scalars, inbound_ref, diag_hbm, off_hbm, low_hbm, diag_ref, off_ref, low_ref, sol_ref, rows_ref, sems
):
    pairs = [(off_hbm.at[h], off_ref), (low_hbm, low_ref), (diag_hbm, diag_ref)]
    dest_ref = scalars[0][1]
    copies = fetch(scalars + pairs, sems)
    finish(copies[: len(scalars)])
    get_off, get_low, get_diag = copies[len(scalars) :]
    nodes, rows, _ = off_ref.shape
    per_node = rows // BR
    lanes = low_ref.shape[2]

    def body(k, _):
        rows_ref[k] = inbound_ref[dest_ref[h, k]]
        return 0

    lax.fori_loop(0, nodes * per_node, body, 0, unroll=32)
    get_off.wait()
    taken = []
    for s in range(nodes):
        block_rows = rows_ref[pl.ds(s * per_node, per_node)].reshape(rows, lanes)
        taken.append(
            lax.dot_general(
                off_ref[s], block_rows, (((0,), (0,)), ((), ())), preferred_element_type=F32
            )
        )
    finish([get_low, get_diag])
    solved = []
    for s in range(nodes):
        solved.append(solve_transposed(whole_diag(diag_ref, s), low_ref[s] - taken[s]))
        sol_ref[s] = solved[s]
    return solved


def upper_kernel(
    h,
    dest_hbm,
    code_hbm,
    inbound_ref,
    diag_hbm,
    off_hbm,
    low_hbm,
    _,
    answer_hbm,
    out_ref,
    dest_ref,
    code_ref,
    diag_ref,
    off_ref,
    low_ref,
    sol_ref,
    rows_ref,
    table_ref,
    sems,
):
    solved = upper_solve(
        h, [(dest_hbm, dest_ref), (code_hbm, code_ref)], inbound_ref, diag_hbm, off_hbm, low_hbm,
        diag_ref, off_ref, low_ref, sol_ref, rows_ref, sems,
    )
    kept = store(sol_ref, answer_hbm.at[h], sems.at[5])
    place_rows(h - 1, solved, code_ref, out_ref, table_ref)
    kept.wait()


def last_kernel(
    dest_hbm,
    inbound_ref,
    diag_hbm,
    off_hbm,
    low_hbm,
    _,
    answer_hbm,
    dest_ref,
    diag_ref,
    off_ref,
    low_ref,
    sol_ref,
    rows_ref,
    sems,
):
    upper_solve(
        0, [(dest_hbm, dest_ref)], inbound_ref, diag_hbm, off_hbm, low_hbm,
        diag_ref, off_ref, low_ref, sol_ref, rows_ref, sems,
    )
    store(sol_ref, answer_hbm.at[0], sems.at[5]).wait()


def whole(x):
    return x, pl.BlockSpec(memory_space=pltpu.VMEM)


def far(x):
    return x, pl.BlockSpec(memory_space=pltpu.HBM)


def anywhere(x):
    return x, pl.BlockSpec(memory_space=pl.ANY)


def call(kernel, name, operands, outs, scratch, flops, aliases={}, limit=None):
    arrays = [x for x, _ in operands]
    moved = sum(x.size * x.dtype.itemsize for x, _ in operands + outs)
    return pl.pallas_call(
        kernel,
        name=name,
        out_shape=[jax.ShapeDtypeStruct(x.shape, x.dtype) for x, _ in outs],
        in_specs=[spec for _, spec in operands],
        out_specs=[spec for _, spec in outs],
        scratch_shapes=scratch,
        input_output_aliases=aliases,
        compiler_params=pltpu.CompilerParams(vmem_limit_bytes=limit),
        cost_estimate=pl.CostEstimate(flops=flops, bytes_accessed=moved, transcendentals=0),
    )(*arrays)


def on_device(right_sides, diag_inverse, off_diagonal, target_snode, target_block):
    levels, nodes, order, lanes = right_sides.shape
    per_node = target_snode.shape[2]
    row_blocks = order // BR
    devices = lax.axis_size("snode")
    sharers = lax.axis_size("rhs")
    outgoing = nodes * per_node
    capacity = CAPACITY
    slots = devices * capacity
    local_rows = nodes * row_blocks
    couplings = levels - 1

    def diag_parts(mine):
        steps = [[(y, (y + k) % sharers) for y in range(sharers)] for k in range(1, sharers)]
        return [lax.ppermute(mine, "rhs", step) for step in steps]

    first_parts = diag_parts(diag_inverse[0])

    block_order = lax.iota(jnp.int32, outgoing)
    flat_target = target_snode.reshape(couplings, outgoing)
    owner = flat_target // nodes
    row = flat_target % nodes * row_blocks + target_block.reshape(couplings, outgoing)
    earlier = (owner[:, :, None] == owner[:, None, :]) & (
        block_order[None, None, :] < block_order[None, :, None]
    )
    destinations = owner * capacity + jnp.sum(earlier.astype(jnp.int32), axis=2)
    slot_ids = lax.iota(jnp.int32, slots)
    placed = destinations[:, None, :] == slot_ids[None, :, None]
    sources = jnp.min(jnp.where(placed, block_order[None, None, :], outgoing), axis=2)
    ids = slot_ids.reshape(devices, 1, capacity, 1)
    placed = destinations[None, :, None, :] == ids
    sent = jnp.min(jnp.where(placed, row[None, :, None, :], local_rows), axis=3)

    def exchange(x):
        return lax.all_to_all(x, "snode", split_axis=0, concat_axis=0, tiled=True)

    vector = far(jax.ShapeDtypeStruct((nodes, order, lanes), F32))
    payload = far(jax.ShapeDtypeStruct((slots, BR, lanes), BF16))
    near_payload = whole(payload[0])
    gathered = far(jax.ShapeDtypeStruct((sharers,) + diag_inverse.shape[1:], F32))
    answer = jax.ShapeDtypeStruct(right_sides.shape, F32)
    six = pltpu.SemaphoreType.DMA((6,))
    source_smem = pltpu.SMEM((couplings, slots), jnp.int32)
    code_smem = pltpu.SMEM((couplings * capacity, devices), jnp.int32)
    dest_smem = pltpu.SMEM((couplings, outgoing), jnp.int32)
    two = pltpu.SemaphoreType.DMA((2,))
    inputs = pltpu.SemaphoreType.DMA((12,))
    vectors = pltpu.VMEM((nodes, order, lanes), F32)
    off_buffer = pltpu.VMEM(off_diagonal.shape[1:], BF16)
    diag_buffer = pltpu.VMEM(gathered[0].shape, F32)
    sums = [pltpu.VMEM((local_rows + 1, BR, lanes), F32)] * 4
    table = pltpu.VMEM((outgoing + 1, BR, lanes), BF16)
    row_table = pltpu.VMEM((local_rows + 1, BR, lanes), BF16)
    rows_scratch = pltpu.VMEM((outgoing, BR, lanes), BF16)
    blocks_buffer = pltpu.VMEM((slots, BR, lanes), BF16)
    send = [blocks_buffer, inputs, two, pltpu.SemaphoreType.DMA((8,))]
    flops = 40 * nodes * order * order * lanes
    small = 24 << 20

    def diag_operands(parts):
        return [far(diag_inverse)] + [far(x) for x in parts]

    lower, whole_diags = [None] * couplings, [None] * couplings
    lower[0], whole_diags[0], out = call(
        first_kernel,
        "first",
        [far(sources)]
        + diag_operands(first_parts)
        + [far(right_sides), far(off_diagonal)],
        [vector, gathered, payload],
        [source_smem, diag_buffer, vectors, off_buffer, vectors, table] + send,
        flops,
    )
    later_diags, out = lax.optimization_barrier((diag_inverse, out))
    later_parts = diag_parts(later_diags[1:])
    pairs_of_rows = capacity * BR // 2
    carried = sent.reshape(devices, 1, 1, couplings * capacity).astype(BF16)
    carried = jnp.pad(carried, ((0, 0), (0, 0), (0, 1), (0, lanes - couplings * capacity)))
    out = jnp.concatenate([out.reshape(devices, pairs_of_rows, 2, lanes), carried], axis=1)
    inbound = exchange(out)
    codes = inbound[:, pairs_of_rows, 0, : couplings * capacity].astype(jnp.int32).T
    inbound = inbound[:, :pairs_of_rows].reshape(slots, BR, lanes)

    for h in range(1, couplings):
        lower[h], whole_diags[h], out = call(
            functools.partial(middle_kernel, h),
            "middle",
            [far(sources), far(codes), far(inbound)]
            + diag_operands(later_parts)
            + [far(right_sides), far(off_diagonal)],
            [vector, gathered, payload],
            sums
            + [source_smem, code_smem, blocks_buffer, diag_buffer, vectors, off_buffer, vectors, table]
            + send,
            flops,
        )
        inbound = exchange(out)
    top = couplings
    answer, out = call(
        functools.partial(top_kernel, top),
        "top",
        [far(codes), far(inbound)]
        + diag_operands(later_parts)
        + [far(right_sides)],
        [far(answer), payload],
        sums + [code_smem, blocks_buffer, diag_buffer, vectors, vectors, row_table] + send,
        flops,
    )
    inbound = exchange(out)
    for h in range(couplings - 1, 0, -1):
        answer, out = call(
            functools.partial(upper_kernel, h),
            "upper",
            [far(destinations), far(codes), whole(inbound), anywhere(whole_diags[h])]
            + [anywhere(off_diagonal), anywhere(lower[h]), anywhere(answer)],
            [anywhere(answer), near_payload],
            [dest_smem, code_smem, diag_buffer, off_buffer, vectors, vectors, rows_scratch, row_table, six],
            flops,
            {6: 0},
            small,
        )
        inbound = exchange(out)
    (answer,) = call(
        last_kernel,
        "last",
        [far(destinations), whole(inbound), anywhere(whole_diags[0])]
        + [anywhere(off_diagonal), anywhere(lower[0]), anywhere(answer)],
        [anywhere(answer)],
        [dest_smem, diag_buffer, off_buffer, vectors, vectors, rows_scratch, six],
        flops,
        {5: 0},
        small,
    )
    return answer


def solution(mesh):
    in_specs = (
        P(None, "snode", None, "rhs"),
        P(None, "snode", "rhs", None),
        P(None, "snode", None, None),
        P(None, "snode", None),
        P(None, "snode", None),
    )
    out_specs = P(None, "snode", None, "rhs")
    return jax.shard_map(
        on_device, mesh=mesh, in_specs=in_specs, out_specs=out_specs, check_vma=False
    )
```

```python
import functools

import jax
import jax.numpy as jnp
from jax import lax
from jax.experimental import pallas as pl
from jax.experimental.pallas import tpu as pltpu
from jax.sharding import PartitionSpec as P

BR = 16
CAPACITY = 2
F32 = jnp.float32
BF16 = jnp.bfloat16
PRECISE = lax.Precision.HIGHEST


def whole_diag(diag_ref, s):
    parts = [diag_ref[y, s] for y in range(diag_ref.shape[0])]
    return jnp.concatenate(parts, axis=0)


def solve(diag, x):
    return lax.dot_general(
        diag, x, (((1,), (0,)), ((), ())), precision=PRECISE, preferred_element_type=F32
    )


def solve_transposed(diag, x):
    return lax.dot_general(
        diag, x, (((0,), (0,)), ((), ())), precision=PRECISE, preferred_element_type=F32
    )


def place(table_ref, index, capacity, staged_ref, out_ref, sems):
    chunks = sems.shape[0]
    peers = out_ref.shape[0] // capacity // chunks
    copies = []
    for c in range(chunks):
        place_chunk(table_ref, index, capacity, staged_ref, c * peers, peers)
        part = pl.ds(c * peers * capacity, peers * capacity)
        copies.append(pltpu.make_async_copy(staged_ref.at[part], out_ref.at[part], sems.at[c]))
        copies[-1].start()
    return copies


def place_chunk(table_ref, index, capacity, out_ref, start, peers):
    def body(d, _):
        for i in range(capacity):
            out_ref[d * capacity + i] = table_ref[index(d, i)]
        return 0

    lax.fori_loop(start, start + peers, body, 0, unroll=16)


def source_index(h, capacity, source_ref):
    return lambda d, i: source_ref[h, d * capacity + i]


def code_index(h, capacity, code_ref):
    return lambda d, i: code_ref[h * capacity + i, d]


def send_updates(h, low_ref, off_ref, source_ref, staged_ref, out_ref, table_ref, sems):
    nodes, rows, _ = off_ref.shape
    lanes = low_ref.shape[2]
    per_node = rows // BR
    for s in range(nodes):
        update = jnp.dot(off_ref[s], low_ref[s].astype(BF16), preferred_element_type=F32)
        table_ref[pl.ds(s * per_node, per_node)] = update.astype(BF16).reshape(per_node, BR, lanes)
    table_ref[nodes * per_node] = jnp.zeros((BR, lanes), BF16)
    index = source_index(h, CAPACITY, source_ref)
    return place(table_ref, index, CAPACITY, staged_ref, out_ref, sems)


def fill_rows(solved, table_ref):
    blocks, _, lanes = table_ref.shape
    per_node = (blocks - 1) // len(solved)
    for s, values in enumerate(solved):
        table_ref[pl.ds(s * per_node, per_node)] = values.astype(BF16).reshape(per_node, BR, lanes)
    table_ref[blocks - 1] = jnp.zeros((BR, lanes), BF16)


def send_rows(h, solved, code_ref, staged_ref, out_ref, table_ref, sems):
    fill_rows(solved, table_ref)
    index = code_index(h, CAPACITY, code_ref)
    return place(table_ref, index, CAPACITY, staged_ref, out_ref, sems)


def place_rows(h, solved, code_ref, out_ref, table_ref):
    fill_rows(solved, table_ref)
    index = code_index(h, CAPACITY, code_ref)
    place_chunk(table_ref, index, CAPACITY, out_ref, 0, out_ref.shape[0] // CAPACITY)


def fetch(pairs, sems):
    copies = [pltpu.make_async_copy(a, b, sems.at[i]) for i, (a, b) in enumerate(pairs)]
    for copy in copies:
        copy.start()
    return copies


def store(source, target, sem):
    copy = pltpu.make_async_copy(source, target, sem)
    copy.start()
    return copy


def finish(copies):
    for copy in copies:
        copy.wait()


def add_blocks(inbound_ref, index, sum_refs, start, peers):
    step = len(sum_refs) // CAPACITY

    def body(g, _):
        for e in range(step):
            d = g * step + e
            for i in range(CAPACITY):
                sum_ref = sum_refs[e * CAPACITY + i]
                code = index(d, i)
                sum_ref[code] = sum_ref[code] + inbound_ref[d * CAPACITY + i].astype(F32)
        return 0

    lax.fori_loop(start // step, (start + peers) // step, body, 0, unroll=4)


def diag_copies(own_hbm, part_hbms, diag_ref):
    sharers = diag_ref.shape[0]
    mine = lax.axis_index("rhs")
    sources = [own_hbm] + list(part_hbms)
    return [
        (source, diag_ref.at[lax.rem(mine + (sharers - i), sharers)])
        for i, source in enumerate(sources)
    ]


def lower_solve(code_hbm, code_ref, inbound_hbm, inbound_ref, index, sum_refs, diag_ref, rhs_ref, others, sems):
    nodes, order, lanes = rhs_ref.shape
    chunks = 4
    size = inbound_ref.shape[0] // chunks
    pairs = []
    for c in range(chunks):
        part = pl.ds(c * size, size)
        pairs.append((inbound_hbm.at[part], inbound_ref.at[part]))
    copies = fetch([(code_hbm, code_ref)] + pairs + others, sems)
    get_code, copies = copies[0], copies[1:]
    for sum_ref in sum_refs:
        sum_ref[...] = jnp.zeros_like(sum_ref)
    get_code.wait()
    for c in range(chunks):
        copies[c].wait()
        add_blocks(inbound_ref, index, sum_refs, c * size // CAPACITY, size // CAPACITY)
    rest = copies[chunks:]
    finish(rest[:NEEDED])
    blocks = order // BR
    solved = []
    for s in range(nodes):
        part = pl.ds(s * blocks, blocks)
        total = sum(sum_ref[part] for sum_ref in sum_refs).reshape(order, lanes)
        solved.append(solve(whole_diag(diag_ref, s), rhs_ref[s] - total))
    return solved, rest[NEEDED:]


NEEDED = 5


def first_kernel(
    source_hbm,
    diag_hbm,
    part1_hbm,
    part2_hbm,
    part3_hbm,
    rhs_hbm,
    off_hbm,
    low_hbm,
    whole_hbm,
    out_hbm,
    source_ref,
    diag_ref,
    rhs_ref,
    off_ref,
    low_ref,
    table_ref,
    staged_ref,
    in_sems,
    keep_sems,
    out_sems,
):
    pairs = diag_copies(diag_hbm.at[0], [part1_hbm, part2_hbm, part3_hbm], diag_ref)
    pairs += [(rhs_hbm.at[0], rhs_ref), (off_hbm.at[0], off_ref), (source_hbm, source_ref)]
    copies = fetch(pairs, in_sems)
    finish(copies[:NEEDED])
    kept = [store(diag_ref, whole_hbm, keep_sems.at[0])]
    for s in range(rhs_ref.shape[0]):
        low_ref[s] = solve(whole_diag(diag_ref, s), rhs_ref[s])
    kept.append(store(low_ref, low_hbm, keep_sems.at[1]))
    finish(copies[NEEDED:])
    kept += send_updates(0, low_ref, off_ref, source_ref, staged_ref, out_hbm, table_ref, out_sems)
    finish(kept)


def middle_kernel(
    h,
    source_hbm,
    code_hbm,
    inbound_hbm,
    diag_hbm,
    part1_hbm,
    part2_hbm,
    part3_hbm,
    rhs_hbm,
    off_hbm,
    low_hbm,
    whole_hbm,
    out_hbm,
    sum0_ref,
    sum1_ref,
    sum2_ref,
    sum3_ref,
    source_ref,
    code_ref,
    inbound_ref,
    diag_ref,
    rhs_ref,
    off_ref,
    low_ref,
    table_ref,
    staged_ref,
    in_sems,
    keep_sems,
    out_sems,
):
    later = [part_hbm.at[h - 1] for part_hbm in (part1_hbm, part2_hbm, part3_hbm)]
    pairs = diag_copies(diag_hbm.at[h], later, diag_ref)
    pairs += [(rhs_hbm.at[h], rhs_ref), (off_hbm.at[h], off_ref), (source_hbm, source_ref)]
    sums = [sum0_ref, sum1_ref, sum2_ref, sum3_ref]
    index = code_index(h - 1, CAPACITY, code_ref)
    solved, late = lower_solve(
        code_hbm, code_ref, inbound_hbm, inbound_ref, index, sums, diag_ref, rhs_ref, pairs, in_sems
    )
    kept = [store(diag_ref, whole_hbm, keep_sems.at[0])]
    for s, values in enumerate(solved):
        low_ref[s] = values
    kept.append(store(low_ref, low_hbm, keep_sems.at[1]))
    finish(late)
    kept += send_updates(h, low_ref, off_ref, source_ref, staged_ref, out_hbm, table_ref, out_sems)
    finish(kept)


def top_kernel(
    h,
    code_hbm,
    inbound_hbm,
    diag_hbm,
    part1_hbm,
    part2_hbm,
    part3_hbm,
    rhs_hbm,
    answer_hbm,
    out_hbm,
    sum0_ref,
    sum1_ref,
    sum2_ref,
    sum3_ref,
    code_ref,
    inbound_ref,
    diag_ref,
    rhs_ref,
    sol_ref,
    table_ref,
    staged_ref,
    in_sems,
    keep_sems,
    out_sems,
):
    later = [part_hbm.at[h - 1] for part_hbm in (part1_hbm, part2_hbm, part3_hbm)]
    pairs = diag_copies(diag_hbm.at[h], later, diag_ref)
    pairs += [(rhs_hbm.at[h], rhs_ref)]
    sums = [sum0_ref, sum1_ref, sum2_ref, sum3_ref]
    index = code_index(h - 1, CAPACITY, code_ref)
    solved, _ = lower_solve(
        code_hbm, code_ref, inbound_hbm, inbound_ref, index, sums, diag_ref, rhs_ref, pairs, in_sems
    )
    for s, lower in enumerate(solved):
        solved[s] = solve_transposed(whole_diag(diag_ref, s), lower)
        sol_ref[s] = solved[s]
    kept = [store(sol_ref, answer_hbm.at[h], keep_sems.at[0])]
    kept += send_rows(h - 1, solved, code_ref, staged_ref, out_hbm, table_ref, out_sems)
    finish(kept)


def upper_solve(
    h, scalars, inbound_ref, diag_hbm, off_hbm, low_hbm, diag_ref, off_ref, low_ref, sol_ref, rows_ref, sems
):
    pairs = [(off_hbm.at[h], off_ref), (low_hbm, low_ref), (diag_hbm, diag_ref)]
    dest_ref = scalars[0][1]
    copies = fetch(scalars + pairs, sems)
    finish(copies[: len(scalars)])
    get_off, get_low, get_diag = copies[len(scalars) :]
    nodes, rows, _ = off_ref.shape
    per_node = rows // BR
    lanes = low_ref.shape[2]

    def body(k, _):
        rows_ref[k] = inbound_ref[dest_ref[h, k]]
        return 0

    lax.fori_loop(0, nodes * per_node, body, 0, unroll=32)
    get_off.wait()
    taken = []
    for s in range(nodes):
        block_rows = rows_ref[pl.ds(s * per_node, per_node)].reshape(rows, lanes)
        taken.append(
            lax.dot_general(
                off_ref[s], block_rows, (((0,), (0,)), ((), ())), preferred_element_type=F32
            )
        )
    finish([get_low, get_diag])
    solved = []
    for s in range(nodes):
        solved.append(solve_transposed(whole_diag(diag_ref, s), low_ref[s] - taken[s]))
        sol_ref[s] = solved[s]
    return solved


def upper_kernel(
    h,
    dest_hbm,
    code_hbm,
    inbound_ref,
    diag_hbm,
    off_hbm,
    low_hbm,
    _,
    answer_hbm,
    out_ref,
    dest_ref,
    code_ref,
    diag_ref,
    off_ref,
    low_ref,
    sol_ref,
    rows_ref,
    table_ref,
    sems,
):
    solved = upper_solve(
        h, [(dest_hbm, dest_ref), (code_hbm, code_ref)], inbound_ref, diag_hbm, off_hbm, low_hbm,
        diag_ref, off_ref, low_ref, sol_ref, rows_ref, sems,
    )
    kept = store(sol_ref, answer_hbm.at[h], sems.at[5])
    place_rows(h - 1, solved, code_ref, out_ref, table_ref)
    kept.wait()


def last_kernel(
    dest_hbm,
    inbound_ref,
    diag_hbm,
    off_hbm,
    low_hbm,
    _,
    answer_hbm,
    dest_ref,
    diag_ref,
    off_ref,
    low_ref,
    sol_ref,
    rows_ref,
    sems,
):
    upper_solve(
        0, [(dest_hbm, dest_ref)], inbound_ref, diag_hbm, off_hbm, low_hbm,
        diag_ref, off_ref, low_ref, sol_ref, rows_ref, sems,
    )
    store(sol_ref, answer_hbm.at[0], sems.at[5]).wait()


def whole(x):
    return x, pl.BlockSpec(memory_space=pltpu.VMEM)


def far(x):
    return x, pl.BlockSpec(memory_space=pltpu.HBM)


def anywhere(x):
    return x, pl.BlockSpec(memory_space=pl.ANY)


def call(kernel, operands, outs, scratch, flops, aliases={}, limit=None):
    arrays = [x for x, _ in operands]
    moved = sum(x.size * x.dtype.itemsize for x, _ in operands + outs)
    return pl.pallas_call(
        kernel,
        out_shape=[jax.ShapeDtypeStruct(x.shape, x.dtype) for x, _ in outs],
        in_specs=[spec for _, spec in operands],
        out_specs=[spec for _, spec in outs],
        scratch_shapes=scratch,
        input_output_aliases=aliases,
        compiler_params=pltpu.CompilerParams(vmem_limit_bytes=limit),
        cost_estimate=pl.CostEstimate(flops=flops, bytes_accessed=moved, transcendentals=0),
    )(*arrays)


def on_device(right_sides, diag_inverse, off_diagonal, target_snode, target_block):
    levels, nodes, order, lanes = right_sides.shape
    per_node = target_snode.shape[2]
    row_blocks = order // BR
    devices = lax.axis_size("snode")
    sharers = lax.axis_size("rhs")
    outgoing = nodes * per_node
    capacity = CAPACITY
    slots = devices * capacity
    local_rows = nodes * row_blocks
    couplings = levels - 1

    def diag_parts(mine):
        steps = [[(y, (y + k) % sharers) for y in range(sharers)] for k in range(1, sharers)]
        return [lax.ppermute(mine, "rhs", step) for step in steps]

    block_order = lax.iota(jnp.int32, outgoing)
    flat_target = target_snode.reshape(couplings, outgoing)
    owner = flat_target // nodes
    row = flat_target % nodes * row_blocks + target_block.reshape(couplings, outgoing)
    earlier = (owner[:, :, None] == owner[:, None, :]) & (
        block_order[None, None, :] < block_order[None, :, None]
    )
    destinations = owner * capacity + jnp.sum(earlier.astype(jnp.int32), axis=2)
    slot_ids = lax.iota(jnp.int32, slots)
    placed = destinations[:, None, :] == slot_ids[None, :, None]
    sources = jnp.min(jnp.where(placed, block_order[None, None, :], outgoing), axis=2)
    ids = slot_ids.reshape(devices, 1, capacity, 1)
    placed = destinations[None, :, None, :] == ids
    sent = jnp.min(jnp.where(placed, row[None, :, None, :], local_rows), axis=3)

    def exchange(x):
        return lax.all_to_all(x, "snode", split_axis=0, concat_axis=0, tiled=True)

    arrived = exchange(sent.reshape(devices, couplings * capacity))
    first_parts = diag_parts(diag_inverse[0])
    codes = arrived.T

    vector = far(jax.ShapeDtypeStruct((nodes, order, lanes), F32))
    payload = far(jax.ShapeDtypeStruct((slots, BR, lanes), BF16))
    near_payload = whole(payload[0])
    gathered = far(jax.ShapeDtypeStruct((sharers,) + diag_inverse.shape[1:], F32))
    answer = jax.ShapeDtypeStruct(right_sides.shape, F32)
    six = pltpu.SemaphoreType.DMA((6,))
    source_smem = pltpu.SMEM((couplings, slots), jnp.int32)
    code_smem = pltpu.SMEM((couplings * capacity, devices), jnp.int32)
    dest_smem = pltpu.SMEM((couplings, outgoing), jnp.int32)
    two = pltpu.SemaphoreType.DMA((2,))
    inputs = pltpu.SemaphoreType.DMA((12,))
    vectors = pltpu.VMEM((nodes, order, lanes), F32)
    off_buffer = pltpu.VMEM(off_diagonal.shape[1:], BF16)
    diag_buffer = pltpu.VMEM(gathered[0].shape, F32)
    sums = [pltpu.VMEM((local_rows + 1, BR, lanes), F32)] * 4
    table = pltpu.VMEM((outgoing + 1, BR, lanes), BF16)
    row_table = pltpu.VMEM((local_rows + 1, BR, lanes), BF16)
    rows_scratch = pltpu.VMEM((outgoing, BR, lanes), BF16)
    blocks_buffer = pltpu.VMEM((slots, BR, lanes), BF16)
    send = [blocks_buffer, inputs, two, pltpu.SemaphoreType.DMA((8,))]
    flops = 40 * nodes * order * order * lanes
    small = 24 << 20

    def diag_operands(parts):
        return [far(diag_inverse)] + [far(x) for x in parts]

    lower, whole_diags = [None] * couplings, [None] * couplings
    lower[0], whole_diags[0], out = call(
        first_kernel,
        [far(sources)]
        + diag_operands(first_parts)
        + [far(right_sides), far(off_diagonal)],
        [vector, gathered, payload],
        [source_smem, diag_buffer, vectors, off_buffer, vectors, table] + send,
        flops,
    )
    later_diags, out = lax.optimization_barrier((diag_inverse, out))
    later_parts = diag_parts(later_diags[1:])
    inbound = exchange(out)

    for h in range(1, couplings):
        lower[h], whole_diags[h], out = call(
            functools.partial(middle_kernel, h),
            [far(sources), far(codes), far(inbound)]
            + diag_operands(later_parts)
            + [far(right_sides), far(off_diagonal)],
            [vector, gathered, payload],
            sums
            + [source_smem, code_smem, blocks_buffer, diag_buffer, vectors, off_buffer, vectors, table]
            + send,
            flops,
        )
        inbound = exchange(out)
    top = couplings
    answer, out = call(
        functools.partial(top_kernel, top),
        [far(codes), far(inbound)]
        + diag_operands(later_parts)
        + [far(right_sides)],
        [far(answer), payload],
        sums + [code_smem, blocks_buffer, diag_buffer, vectors, vectors, row_table] + send,
        flops,
    )
    inbound = exchange(out)
    for h in range(couplings - 1, 0, -1):
        answer, out = call(
            functools.partial(upper_kernel, h),
            [far(destinations), far(codes), whole(inbound), anywhere(whole_diags[h])]
            + [anywhere(off_diagonal), anywhere(lower[h]), anywhere(answer)],
            [anywhere(answer), near_payload],
            [dest_smem, code_smem, diag_buffer, off_buffer, vectors, vectors, rows_scratch, row_table, six],
            flops,
            {6: 0},
            small,
        )
        inbound = exchange(out)
    (answer,) = call(
        last_kernel,
        [far(destinations), whole(inbound), anywhere(whole_diags[0])]
        + [anywhere(off_diagonal), anywhere(lower[0]), anywhere(answer)],
        [anywhere(answer)],
        [dest_smem, diag_buffer, off_buffer, vectors, vectors, rows_scratch, six],
        flops,
        {5: 0},
        small,
    )
    return answer


def solution(mesh):
    in_specs = (
        P(None, "snode", None, "rhs"),
        P(None, "snode", "rhs", None),
        P(None, "snode", None, None),
        P(None, "snode", None),
        P(None, "snode", None),
    )
    out_specs = P(None, "snode", None, "rhs")
    return jax.shard_map(
        on_device, mesh=mesh, in_specs=in_specs, out_specs=out_specs, check_vma=False
    )
```

```python
import functools

import jax
import jax.numpy as jnp
from jax import lax
from jax.experimental import pallas as pl
from jax.experimental.pallas import tpu as pltpu
from jax.sharding import PartitionSpec as P

BR = 16
CAPACITY = 2
F32 = jnp.float32
BF16 = jnp.bfloat16


def whole_diag(diag_ref, s):
    parts = [diag_ref[y, s] for y in range(diag_ref.shape[0])]
    return jnp.concatenate(parts, axis=0)


def halves(x):
    high = x.astype(BF16)
    return high, (x - high.astype(F32)).astype(BF16)


def three_products(diag, x, side):
    dims = (((side,), (0,)), ((), ()))
    (high, low), (x_high, x_low) = halves(diag), halves(x)

    def dot(a, b):
        return lax.dot_general(a, b, dims, preferred_element_type=F32)

    return dot(high, x_high) + (dot(high, x_low) + dot(low, x_high))


def solve(diag, x):
    return three_products(diag, x, 1)


def solve_transposed(diag, x):
    return three_products(diag, x, 0)


def place(table_ref, index, capacity, staged_ref, out_ref, sems):
    chunks = sems.shape[0]
    peers = out_ref.shape[0] // capacity // chunks
    copies = []
    for c in range(chunks):
        place_chunk(table_ref, index, capacity, staged_ref, c * peers, peers)
        part = pl.ds(c * peers * capacity, peers * capacity)
        copies.append(pltpu.make_async_copy(staged_ref.at[part], out_ref.at[part], sems.at[c]))
        copies[-1].start()
    return copies


def place_chunk(table_ref, index, capacity, out_ref, start, peers):
    def body(d, _):
        for i in range(capacity):
            out_ref[d * capacity + i] = table_ref[index(d, i)]
        return 0

    lax.fori_loop(start, start + peers, body, 0, unroll=16)


def source_index(h, capacity, source_ref):
    return lambda d, i: source_ref[h, d * capacity + i]


def code_index(h, capacity, code_ref):
    return lambda d, i: code_ref[h * capacity + i, d]


def send_updates(h, low_ref, off_ref, source_ref, staged_ref, out_ref, table_ref, sems):
    nodes, rows, _ = off_ref.shape
    lanes = low_ref.shape[2]
    per_node = rows // BR
    for s in range(nodes):
        update = jnp.dot(off_ref[s], low_ref[s].astype(BF16), preferred_element_type=F32)
        table_ref[pl.ds(s * per_node, per_node)] = update.astype(BF16).reshape(per_node, BR, lanes)
    table_ref[nodes * per_node] = jnp.zeros((BR, lanes), BF16)
    index = source_index(h, CAPACITY, source_ref)
    return place(table_ref, index, CAPACITY, staged_ref, out_ref, sems)


def fill_rows(solved, table_ref):
    blocks, _, lanes = table_ref.shape
    per_node = (blocks - 1) // len(solved)
    for s, values in enumerate(solved):
        table_ref[pl.ds(s * per_node, per_node)] = values.astype(BF16).reshape(per_node, BR, lanes)
    table_ref[blocks - 1] = jnp.zeros((BR, lanes), BF16)


def send_rows(h, solved, code_ref, staged_ref, out_ref, table_ref, sems):
    fill_rows(solved, table_ref)
    index = code_index(h, CAPACITY, code_ref)
    return place(table_ref, index, CAPACITY, staged_ref, out_ref, sems)


def place_rows(h, solved, code_ref, out_ref, table_ref):
    fill_rows(solved, table_ref)
    index = code_index(h, CAPACITY, code_ref)
    place_chunk(table_ref, index, CAPACITY, out_ref, 0, out_ref.shape[0] // CAPACITY)


def fetch(pairs, sems):
    copies = [pltpu.make_async_copy(a, b, sems.at[i]) for i, (a, b) in enumerate(pairs)]
    for copy in copies:
        copy.start()
    return copies


def store(source, target, sem):
    copy = pltpu.make_async_copy(source, target, sem)
    copy.start()
    return copy


def finish(copies):
    for copy in copies:
        copy.wait()


def add_blocks(inbound_ref, index, sum_refs, start, peers):
    step = len(sum_refs) // CAPACITY

    def body(g, _):
        for e in range(step):
            d = g * step + e
            for i in range(CAPACITY):
                sum_ref = sum_refs[e * CAPACITY + i]
                code = index(d, i)
                sum_ref[code] = sum_ref[code] + inbound_ref[d * CAPACITY + i].astype(F32)
        return 0

    lax.fori_loop(start // step, (start + peers) // step, body, 0, unroll=4)


def diag_copies(own_hbm, part_hbms, diag_ref):
    sharers = diag_ref.shape[0]
    mine = lax.axis_index("rhs")
    sources = [own_hbm] + list(part_hbms)
    return [
        (source, diag_ref.at[lax.rem(mine + (sharers - i), sharers)])
        for i, source in enumerate(sources)
    ]


def lower_solve(code_hbm, code_ref, inbound_hbm, inbound_ref, index, sum_refs, diag_ref, rhs_ref, others, sems):
    nodes, order, lanes = rhs_ref.shape
    chunks = 4
    size = inbound_ref.shape[0] // chunks
    pairs = []
    for c in range(chunks):
        part = pl.ds(c * size, size)
        pairs.append((inbound_hbm.at[part], inbound_ref.at[part]))
    copies = fetch([(code_hbm, code_ref)] + pairs + others, sems)
    get_code, copies = copies[0], copies[1:]
    for sum_ref in sum_refs:
        sum_ref[...] = jnp.zeros_like(sum_ref)
    get_code.wait()
    for c in range(chunks):
        copies[c].wait()
        add_blocks(inbound_ref, index, sum_refs, c * size // CAPACITY, size // CAPACITY)
    rest = copies[chunks:]
    finish(rest[:NEEDED])
    blocks = order // BR
    solved = []
    for s in range(nodes):
        part = pl.ds(s * blocks, blocks)
        total = sum(sum_ref[part] for sum_ref in sum_refs).reshape(order, lanes)
        solved.append(solve(whole_diag(diag_ref, s), rhs_ref[s] - total))
    return solved, rest[NEEDED:]


NEEDED = 5


def first_kernel(
    source_hbm,
    diag_hbm,
    part1_hbm,
    part2_hbm,
    part3_hbm,
    rhs_hbm,
    off_hbm,
    low_hbm,
    whole_hbm,
    out_hbm,
    source_ref,
    diag_ref,
    rhs_ref,
    off_ref,
    low_ref,
    table_ref,
    staged_ref,
    in_sems,
    keep_sems,
    out_sems,
):
    pairs = diag_copies(diag_hbm.at[0], [part1_hbm, part2_hbm, part3_hbm], diag_ref)
    pairs += [(rhs_hbm.at[0], rhs_ref), (off_hbm.at[0], off_ref), (source_hbm, source_ref)]
    copies = fetch(pairs, in_sems)
    finish(copies[:NEEDED])
    kept = [store(diag_ref, whole_hbm, keep_sems.at[0])]
    for s in range(rhs_ref.shape[0]):
        low_ref[s] = solve(whole_diag(diag_ref, s), rhs_ref[s])
    kept.append(store(low_ref, low_hbm, keep_sems.at[1]))
    finish(copies[NEEDED:])
    kept += send_updates(0, low_ref, off_ref, source_ref, staged_ref, out_hbm, table_ref, out_sems)
    finish(kept)


def middle_kernel(
    h,
    source_hbm,
    code_hbm,
    inbound_hbm,
    diag_hbm,
    part1_hbm,
    part2_hbm,
    part3_hbm,
    rhs_hbm,
    off_hbm,
    low_hbm,
    whole_hbm,
    out_hbm,
    sum0_ref,
    sum1_ref,
    sum2_ref,
    sum3_ref,
    source_ref,
    code_ref,
    inbound_ref,
    diag_ref,
    rhs_ref,
    off_ref,
    low_ref,
    table_ref,
    staged_ref,
    in_sems,
    keep_sems,
    out_sems,
):
    later = [part_hbm.at[h - 1] for part_hbm in (part1_hbm, part2_hbm, part3_hbm)]
    pairs = diag_copies(diag_hbm.at[h], later, diag_ref)
    pairs += [(rhs_hbm.at[h], rhs_ref), (off_hbm.at[h], off_ref), (source_hbm, source_ref)]
    sums = [sum0_ref, sum1_ref, sum2_ref, sum3_ref]
    index = code_index(h - 1, CAPACITY, code_ref)
    solved, late = lower_solve(
        code_hbm, code_ref, inbound_hbm, inbound_ref, index, sums, diag_ref, rhs_ref, pairs, in_sems
    )
    kept = [store(diag_ref, whole_hbm, keep_sems.at[0])]
    for s, values in enumerate(solved):
        low_ref[s] = values
    kept.append(store(low_ref, low_hbm, keep_sems.at[1]))
    finish(late)
    kept += send_updates(h, low_ref, off_ref, source_ref, staged_ref, out_hbm, table_ref, out_sems)
    finish(kept)


def top_kernel(
    h,
    code_hbm,
    inbound_hbm,
    diag_hbm,
    part1_hbm,
    part2_hbm,
    part3_hbm,
    rhs_hbm,
    answer_hbm,
    out_hbm,
    sum0_ref,
    sum1_ref,
    sum2_ref,
    sum3_ref,
    code_ref,
    inbound_ref,
    diag_ref,
    rhs_ref,
    sol_ref,
    table_ref,
    staged_ref,
    in_sems,
    keep_sems,
    out_sems,
):
    later = [part_hbm.at[h - 1] for part_hbm in (part1_hbm, part2_hbm, part3_hbm)]
    pairs = diag_copies(diag_hbm.at[h], later, diag_ref)
    pairs += [(rhs_hbm.at[h], rhs_ref)]
    sums = [sum0_ref, sum1_ref, sum2_ref, sum3_ref]
    index = code_index(h - 1, CAPACITY, code_ref)
    solved, _ = lower_solve(
        code_hbm, code_ref, inbound_hbm, inbound_ref, index, sums, diag_ref, rhs_ref, pairs, in_sems
    )
    for s, lower in enumerate(solved):
        solved[s] = solve_transposed(whole_diag(diag_ref, s), lower)
        sol_ref[s] = solved[s]
    kept = [store(sol_ref, answer_hbm.at[h], keep_sems.at[0])]
    kept += send_rows(h - 1, solved, code_ref, staged_ref, out_hbm, table_ref, out_sems)
    finish(kept)


def upper_solve(
    h, scalars, inbound_ref, diag_hbm, off_hbm, low_hbm, diag_ref, off_ref, low_ref, sol_ref, rows_ref, sems
):
    pairs = [(off_hbm.at[h], off_ref), (low_hbm, low_ref), (diag_hbm, diag_ref)]
    dest_ref = scalars[0][1]
    copies = fetch(scalars + pairs, sems)
    finish(copies[: len(scalars)])
    get_off, get_low, get_diag = copies[len(scalars) :]
    nodes, rows, _ = off_ref.shape
    per_node = rows // BR
    lanes = low_ref.shape[2]

    def body(k, _):
        rows_ref[k] = inbound_ref[dest_ref[h, k]]
        return 0

    lax.fori_loop(0, nodes * per_node, body, 0, unroll=32)
    get_off.wait()
    taken = []
    for s in range(nodes):
        block_rows = rows_ref[pl.ds(s * per_node, per_node)].reshape(rows, lanes)
        taken.append(
            lax.dot_general(
                off_ref[s], block_rows, (((0,), (0,)), ((), ())), preferred_element_type=F32
            )
        )
    finish([get_low, get_diag])
    solved = []
    for s in range(nodes):
        solved.append(solve_transposed(whole_diag(diag_ref, s), low_ref[s] - taken[s]))
        sol_ref[s] = solved[s]
    return solved


def upper_kernel(
    h,
    dest_hbm,
    code_hbm,
    inbound_ref,
    diag_hbm,
    off_hbm,
    low_hbm,
    _,
    answer_hbm,
    out_ref,
    dest_ref,
    code_ref,
    diag_ref,
    off_ref,
    low_ref,
    sol_ref,
    rows_ref,
    table_ref,
    sems,
):
    solved = upper_solve(
        h, [(dest_hbm, dest_ref), (code_hbm, code_ref)], inbound_ref, diag_hbm, off_hbm, low_hbm,
        diag_ref, off_ref, low_ref, sol_ref, rows_ref, sems,
    )
    kept = store(sol_ref, answer_hbm.at[h], sems.at[5])
    place_rows(h - 1, solved, code_ref, out_ref, table_ref)
    kept.wait()


def last_kernel(
    dest_hbm,
    inbound_ref,
    diag_hbm,
    off_hbm,
    low_hbm,
    _,
    answer_hbm,
    dest_ref,
    diag_ref,
    off_ref,
    low_ref,
    sol_ref,
    rows_ref,
    sems,
):
    upper_solve(
        0, [(dest_hbm, dest_ref)], inbound_ref, diag_hbm, off_hbm, low_hbm,
        diag_ref, off_ref, low_ref, sol_ref, rows_ref, sems,
    )
    store(sol_ref, answer_hbm.at[0], sems.at[5]).wait()


def whole(x):
    return x, pl.BlockSpec(memory_space=pltpu.VMEM)


def far(x):
    return x, pl.BlockSpec(memory_space=pltpu.HBM)


def anywhere(x):
    return x, pl.BlockSpec(memory_space=pl.ANY)


def call(kernel, name, operands, outs, scratch, flops, aliases={}, limit=None):
    arrays = [x for x, _ in operands]
    moved = sum(x.size * x.dtype.itemsize for x, _ in operands + outs)
    return pl.pallas_call(
        kernel,
        name=name,
        out_shape=[jax.ShapeDtypeStruct(x.shape, x.dtype) for x, _ in outs],
        in_specs=[spec for _, spec in operands],
        out_specs=[spec for _, spec in outs],
        scratch_shapes=scratch,
        input_output_aliases=aliases,
        compiler_params=pltpu.CompilerParams(vmem_limit_bytes=limit),
        cost_estimate=pl.CostEstimate(flops=flops, bytes_accessed=moved, transcendentals=0),
    )(*arrays)


def on_device(right_sides, diag_inverse, off_diagonal, target_snode, target_block):
    levels, nodes, order, lanes = right_sides.shape
    per_node = target_snode.shape[2]
    row_blocks = order // BR
    devices = lax.axis_size("snode")
    sharers = lax.axis_size("rhs")
    outgoing = nodes * per_node
    capacity = CAPACITY
    slots = devices * capacity
    local_rows = nodes * row_blocks
    couplings = levels - 1

    def diag_parts(mine):
        steps = [[(y, (y + k) % sharers) for y in range(sharers)] for k in range(1, sharers)]
        return [lax.ppermute(mine, "rhs", step) for step in steps]

    first_parts = diag_parts(diag_inverse[0])

    block_order = lax.iota(jnp.int32, outgoing)
    flat_target = target_snode.reshape(couplings, outgoing)
    owner = flat_target // nodes
    row = flat_target % nodes * row_blocks + target_block.reshape(couplings, outgoing)
    earlier = (owner[:, :, None] == owner[:, None, :]) & (
        block_order[None, None, :] < block_order[None, :, None]
    )
    destinations = owner * capacity + jnp.sum(earlier.astype(jnp.int32), axis=2)
    slot_ids = lax.iota(jnp.int32, slots)
    placed = destinations[:, None, :] == slot_ids[None, :, None]
    sources = jnp.min(jnp.where(placed, block_order[None, None, :], outgoing), axis=2)
    ids = slot_ids.reshape(devices, 1, capacity, 1)
    placed = destinations[None, :, None, :] == ids
    sent = jnp.min(jnp.where(placed, row[None, :, None, :], local_rows), axis=3)

    def exchange(x):
        return lax.all_to_all(x, "snode", split_axis=0, concat_axis=0, tiled=True)

    vector = far(jax.ShapeDtypeStruct((nodes, order, lanes), F32))
    payload = far(jax.ShapeDtypeStruct((slots, BR, lanes), BF16))
    near_payload = whole(payload[0])
    gathered = far(jax.ShapeDtypeStruct((sharers,) + diag_inverse.shape[1:], F32))
    answer = jax.ShapeDtypeStruct(right_sides.shape, F32)
    six = pltpu.SemaphoreType.DMA((6,))
    source_smem = pltpu.SMEM((couplings, slots), jnp.int32)
    code_smem = pltpu.SMEM((couplings * capacity, devices), jnp.int32)
    dest_smem = pltpu.SMEM((couplings, outgoing), jnp.int32)
    two = pltpu.SemaphoreType.DMA((2,))
    inputs = pltpu.SemaphoreType.DMA((12,))
    vectors = pltpu.VMEM((nodes, order, lanes), F32)
    off_buffer = pltpu.VMEM(off_diagonal.shape[1:], BF16)
    diag_buffer = pltpu.VMEM(gathered[0].shape, F32)
    sums = [pltpu.VMEM((local_rows + 1, BR, lanes), F32)] * 4
    table = pltpu.VMEM((outgoing + 1, BR, lanes), BF16)
    row_table = pltpu.VMEM((local_rows + 1, BR, lanes), BF16)
    rows_scratch = pltpu.VMEM((outgoing, BR, lanes), BF16)
    blocks_buffer = pltpu.VMEM((slots, BR, lanes), BF16)
    send = [blocks_buffer, inputs, two, pltpu.SemaphoreType.DMA((8,))]
    flops = 40 * nodes * order * order * lanes
    small = 24 << 20

    def diag_operands(parts):
        return [far(diag_inverse)] + [far(x) for x in parts]

    lower, whole_diags = [None] * couplings, [None] * couplings
    lower[0], whole_diags[0], out = call(
        first_kernel,
        "first",
        [far(sources)]
        + diag_operands(first_parts)
        + [far(right_sides), far(off_diagonal)],
        [vector, gathered, payload],
        [source_smem, diag_buffer, vectors, off_buffer, vectors, table] + send,
        flops,
    )
    later_diags, out = lax.optimization_barrier((diag_inverse, out))
    later_parts = diag_parts(later_diags[1:])
    pairs_of_rows = capacity * BR // 2
    carried = sent.reshape(devices, 1, 1, couplings * capacity).astype(BF16)
    carried = jnp.pad(carried, ((0, 0), (0, 0), (0, 1), (0, lanes - couplings * capacity)))
    out = jnp.concatenate([out.reshape(devices, pairs_of_rows, 2, lanes), carried], axis=1)
    inbound = exchange(out)
    codes = inbound[:, pairs_of_rows, 0, : couplings * capacity].astype(jnp.int32).T
    inbound = inbound[:, :pairs_of_rows].reshape(slots, BR, lanes)

    for h in range(1, couplings):
        lower[h], whole_diags[h], out = call(
            functools.partial(middle_kernel, h),
            "middle",
            [far(sources), far(codes), far(inbound)]
            + diag_operands(later_parts)
            + [far(right_sides), far(off_diagonal)],
            [vector, gathered, payload],
            sums
            + [source_smem, code_smem, blocks_buffer, diag_buffer, vectors, off_buffer, vectors, table]
            + send,
            flops,
        )
        inbound = exchange(out)
    top = couplings
    answer, out = call(
        functools.partial(top_kernel, top),
        "top",
        [far(codes), far(inbound)]
        + diag_operands(later_parts)
        + [far(right_sides)],
        [far(answer), payload],
        sums + [code_smem, blocks_buffer, diag_buffer, vectors, vectors, row_table] + send,
        flops,
    )
    inbound = exchange(out)
    for h in range(couplings - 1, 0, -1):
        answer, out = call(
            functools.partial(upper_kernel, h),
            "upper",
            [far(destinations), far(codes), whole(inbound), anywhere(whole_diags[h])]
            + [anywhere(off_diagonal), anywhere(lower[h]), anywhere(answer)],
            [anywhere(answer), near_payload],
            [dest_smem, code_smem, diag_buffer, off_buffer, vectors, vectors, rows_scratch, row_table, six],
            flops,
            {6: 0},
            small,
        )
        inbound = exchange(out)
    (answer,) = call(
        last_kernel,
        "last",
        [far(destinations), whole(inbound), anywhere(whole_diags[0])]
        + [anywhere(off_diagonal), anywhere(lower[0]), anywhere(answer)],
        [anywhere(answer)],
        [dest_smem, diag_buffer, off_buffer, vectors, vectors, rows_scratch, six],
        flops,
        {5: 0},
        small,
    )
    return answer


def solution(mesh):
    in_specs = (
        P(None, "snode", None, "rhs"),
        P(None, "snode", "rhs", None),
        P(None, "snode", None, None),
        P(None, "snode", None),
        P(None, "snode", None),
    )
    out_specs = P(None, "snode", None, "rhs")
    return jax.shard_map(
        on_device, mesh=mesh, in_specs=in_specs, out_specs=out_specs, check_vma=False
    )
```

```python
import functools

import jax
import jax.numpy as jnp
from jax import lax
from jax.experimental import pallas as pl
from jax.experimental.pallas import tpu as pltpu
from jax.sharding import PartitionSpec as P

BR = 16
CAPACITY = 2
F32 = jnp.float32
BF16 = jnp.bfloat16


def whole_diag(diag_ref, s):
    parts = [diag_ref[y, s] for y in range(diag_ref.shape[0])]
    return jnp.concatenate(parts, axis=0)


def halves(x):
    high = x.astype(BF16)
    return high, (x - high.astype(F32)).astype(BF16)


def three_products(diag, x, side):
    dims = (((side,), (0,)), ((), ()))
    (high, low), (x_high, x_low) = halves(diag), halves(x)

    def dot(a, b):
        return lax.dot_general(a, b, dims, preferred_element_type=F32)

    return dot(high, x_high) + (dot(high, x_low) + dot(low, x_high))


def solve(diag, x):
    return three_products(diag, x, 1)


def solve_transposed(diag, x):
    return three_products(diag, x, 0)


def place(table_ref, index, capacity, staged_ref, out_ref, sems):
    chunks = sems.shape[0]
    peers = out_ref.shape[0] // capacity // chunks
    copies = []
    for c in range(chunks):
        place_chunk(table_ref, index, capacity, staged_ref, c * peers, peers)
        part = pl.ds(c * peers * capacity, peers * capacity)
        copies.append(pltpu.make_async_copy(staged_ref.at[part], out_ref.at[part], sems.at[c]))
        copies[-1].start()
    return copies


def place_chunk(table_ref, index, capacity, out_ref, start, peers):
    def body(d, _):
        for i in range(capacity):
            out_ref[d * capacity + i] = table_ref[index(d, i)]
        return 0

    lax.fori_loop(start, start + peers, body, 0, unroll=16)


def source_index(h, capacity, source_ref):
    return lambda d, i: source_ref[h, d * capacity + i]


def code_index(h, capacity, code_ref):
    return lambda d, i: code_ref[h * capacity + i, d]


def send_updates(h, low_ref, off_ref, source_ref, staged_ref, out_ref, table_ref, sems):
    nodes, rows, _ = off_ref.shape
    lanes = low_ref.shape[2]
    per_node = rows // BR
    for s in range(nodes):
        update = jnp.dot(off_ref[s], low_ref[s].astype(BF16), preferred_element_type=F32)
        table_ref[pl.ds(s * per_node, per_node)] = update.astype(BF16).reshape(per_node, BR, lanes)
    table_ref[nodes * per_node] = jnp.zeros((BR, lanes), BF16)
    index = source_index(h, CAPACITY, source_ref)
    return place(table_ref, index, CAPACITY, staged_ref, out_ref, sems)


def fill_rows(solved, table_ref):
    blocks, _, lanes = table_ref.shape
    per_node = (blocks - 1) // len(solved)
    for s, values in enumerate(solved):
        table_ref[pl.ds(s * per_node, per_node)] = values.astype(BF16).reshape(per_node, BR, lanes)
    table_ref[blocks - 1] = jnp.zeros((BR, lanes), BF16)


def send_rows(h, solved, code_ref, staged_ref, out_ref, table_ref, sems):
    fill_rows(solved, table_ref)
    index = code_index(h, CAPACITY, code_ref)
    return place(table_ref, index, CAPACITY, staged_ref, out_ref, sems)


def place_rows(h, solved, code_ref, out_ref, table_ref):
    fill_rows(solved, table_ref)
    index = code_index(h, CAPACITY, code_ref)
    place_chunk(table_ref, index, CAPACITY, out_ref, 0, out_ref.shape[0] // CAPACITY)


def fetch(pairs, sems):
    copies = [pltpu.make_async_copy(a, b, sems.at[i]) for i, (a, b) in enumerate(pairs)]
    for copy in copies:
        copy.start()
    return copies


def store(source, target, sem):
    copy = pltpu.make_async_copy(source, target, sem)
    copy.start()
    return copy


def finish(copies):
    for copy in copies:
        copy.wait()


def add_blocks(inbound_ref, index, sum_refs, start, peers):
    step = len(sum_refs) // CAPACITY

    def body(g, _):
        for e in range(step):
            d = g * step + e
            for i in range(CAPACITY):
                sum_ref = sum_refs[e * CAPACITY + i]
                code = index(d, i)
                sum_ref[code] = sum_ref[code] + inbound_ref[d * CAPACITY + i].astype(F32)
        return 0

    lax.fori_loop(start // step, (start + peers) // step, body, 0, unroll=4)


def shift_order(sharers):
    return sorted(range(sharers), key=lambda k: min(k, sharers - k))


def diag_copies(own_hbm, part_hbms, diag_ref):
    sharers = diag_ref.shape[0]
    mine = lax.axis_index("rhs")
    sources = [own_hbm] + list(part_hbms)
    return [
        (source, diag_ref.at[lax.rem(mine + (sharers - i), sharers)])
        for i, source in zip(shift_order(sharers), sources)
    ]


def lower_solve(code_hbm, code_ref, inbound_hbm, inbound_ref, index, sum_refs, diag_ref, rhs_ref, others, sems):
    nodes, order, lanes = rhs_ref.shape
    chunks = 4
    size = inbound_ref.shape[0] // chunks
    pairs = []
    for c in range(chunks):
        part = pl.ds(c * size, size)
        pairs.append((inbound_hbm.at[part], inbound_ref.at[part]))
    copies = fetch([(code_hbm, code_ref)] + pairs + others, sems)
    get_code, copies = copies[0], copies[1:]
    for sum_ref in sum_refs:
        sum_ref[...] = jnp.zeros_like(sum_ref)
    get_code.wait()
    for c in range(chunks):
        copies[c].wait()
        add_blocks(inbound_ref, index, sum_refs, c * size // CAPACITY, size // CAPACITY)
    rest = copies[chunks:]
    finish(rest[:NEEDED])
    blocks = order // BR
    solved = []
    for s in range(nodes):
        part = pl.ds(s * blocks, blocks)
        total = sum(sum_ref[part] for sum_ref in sum_refs).reshape(order, lanes)
        solved.append(solve(whole_diag(diag_ref, s), rhs_ref[s] - total))
    return solved, rest[NEEDED:]


NEEDED = 5


def first_kernel(
    source_hbm,
    diag_hbm,
    part1_hbm,
    part2_hbm,
    part3_hbm,
    rhs_hbm,
    off_hbm,
    low_hbm,
    whole_hbm,
    out_hbm,
    source_ref,
    diag_ref,
    rhs_ref,
    off_ref,
    low_ref,
    table_ref,
    staged_ref,
    in_sems,
    keep_sems,
    out_sems,
):
    pairs = diag_copies(diag_hbm.at[0], [part1_hbm, part2_hbm, part3_hbm], diag_ref)
    pairs += [(rhs_hbm.at[0], rhs_ref), (off_hbm.at[0], off_ref), (source_hbm, source_ref)]
    copies = fetch(pairs, in_sems)
    finish(copies[:NEEDED])
    kept = [store(diag_ref, whole_hbm, keep_sems.at[0])]
    for s in range(rhs_ref.shape[0]):
        low_ref[s] = solve(whole_diag(diag_ref, s), rhs_ref[s])
    kept.append(store(low_ref, low_hbm, keep_sems.at[1]))
    finish(copies[NEEDED:])
    kept += send_updates(0, low_ref, off_ref, source_ref, staged_ref, out_hbm, table_ref, out_sems)
    finish(kept)


def middle_kernel(
    h,
    source_hbm,
    code_hbm,
    inbound_hbm,
    diag_hbm,
    part1_hbm,
    part2_hbm,
    part3_hbm,
    rhs_hbm,
    off_hbm,
    low_hbm,
    whole_hbm,
    out_hbm,
    sum0_ref,
    sum1_ref,
    sum2_ref,
    sum3_ref,
    source_ref,
    code_ref,
    inbound_ref,
    diag_ref,
    rhs_ref,
    off_ref,
    low_ref,
    table_ref,
    staged_ref,
    in_sems,
    keep_sems,
    out_sems,
):
    later = [part_hbm.at[h - 1] for part_hbm in (part1_hbm, part2_hbm, part3_hbm)]
    pairs = diag_copies(diag_hbm.at[h], later, diag_ref)
    pairs += [(rhs_hbm.at[h], rhs_ref), (off_hbm.at[h], off_ref), (source_hbm, source_ref)]
    sums = [sum0_ref, sum1_ref, sum2_ref, sum3_ref]
    index = code_index(h - 1, CAPACITY, code_ref)
    solved, late = lower_solve(
        code_hbm, code_ref, inbound_hbm, inbound_ref, index, sums, diag_ref, rhs_ref, pairs, in_sems
    )
    kept = [store(diag_ref, whole_hbm, keep_sems.at[0])]
    for s, values in enumerate(solved):
        low_ref[s] = values
    kept.append(store(low_ref, low_hbm, keep_sems.at[1]))
    finish(late)
    kept += send_updates(h, low_ref, off_ref, source_ref, staged_ref, out_hbm, table_ref, out_sems)
    finish(kept)


def top_kernel(
    h,
    code_hbm,
    inbound_hbm,
    diag_hbm,
    part1_hbm,
    part2_hbm,
    part3_hbm,
    rhs_hbm,
    answer_hbm,
    out_hbm,
    sum0_ref,
    sum1_ref,
    sum2_ref,
    sum3_ref,
    code_ref,
    inbound_ref,
    diag_ref,
    rhs_ref,
    sol_ref,
    table_ref,
    staged_ref,
    in_sems,
    keep_sems,
    out_sems,
):
    later = [part_hbm.at[h - 1] for part_hbm in (part1_hbm, part2_hbm, part3_hbm)]
    pairs = diag_copies(diag_hbm.at[h], later, diag_ref)
    pairs += [(rhs_hbm.at[h], rhs_ref)]
    sums = [sum0_ref, sum1_ref, sum2_ref, sum3_ref]
    index = code_index(h - 1, CAPACITY, code_ref)
    solved, _ = lower_solve(
        code_hbm, code_ref, inbound_hbm, inbound_ref, index, sums, diag_ref, rhs_ref, pairs, in_sems
    )
    for s, lower in enumerate(solved):
        solved[s] = solve_transposed(whole_diag(diag_ref, s), lower)
        sol_ref[s] = solved[s]
    kept = [store(sol_ref, answer_hbm.at[h], keep_sems.at[0])]
    kept += send_rows(h - 1, solved, code_ref, staged_ref, out_hbm, table_ref, out_sems)
    finish(kept)


def upper_solve(
    h, scalars, inbound_ref, diag_hbm, off_hbm, low_hbm, diag_ref, off_ref, low_ref, sol_ref, rows_ref, sems
):
    pairs = [(off_hbm.at[h], off_ref), (low_hbm, low_ref), (diag_hbm, diag_ref)]
    dest_ref = scalars[0][1]
    copies = fetch(scalars + pairs, sems)
    finish(copies[: len(scalars)])
    get_off, get_low, get_diag = copies[len(scalars) :]
    nodes, rows, _ = off_ref.shape
    per_node = rows // BR
    lanes = low_ref.shape[2]

    def body(k, _):
        rows_ref[k] = inbound_ref[dest_ref[h, k]]
        return 0

    lax.fori_loop(0, nodes * per_node, body, 0, unroll=32)
    get_off.wait()
    taken = []
    for s in range(nodes):
        block_rows = rows_ref[pl.ds(s * per_node, per_node)].reshape(rows, lanes)
        taken.append(
            lax.dot_general(
                off_ref[s], block_rows, (((0,), (0,)), ((), ())), preferred_element_type=F32
            )
        )
    finish([get_low, get_diag])
    solved = []
    for s in range(nodes):
        solved.append(solve_transposed(whole_diag(diag_ref, s), low_ref[s] - taken[s]))
        sol_ref[s] = solved[s]
    return solved


def upper_kernel(
    h,
    dest_hbm,
    code_hbm,
    inbound_ref,
    diag_hbm,
    off_hbm,
    low_hbm,
    _,
    answer_hbm,
    out_ref,
    dest_ref,
    code_ref,
    diag_ref,
    off_ref,
    low_ref,
    sol_ref,
    rows_ref,
    table_ref,
    sems,
):
    solved = upper_solve(
        h, [(dest_hbm, dest_ref), (code_hbm, code_ref)], inbound_ref, diag_hbm, off_hbm, low_hbm,
        diag_ref, off_ref, low_ref, sol_ref, rows_ref, sems,
    )
    kept = store(sol_ref, answer_hbm.at[h], sems.at[5])
    place_rows(h - 1, solved, code_ref, out_ref, table_ref)
    kept.wait()


def last_kernel(
    dest_hbm,
    inbound_ref,
    diag_hbm,
    off_hbm,
    low_hbm,
    _,
    answer_hbm,
    dest_ref,
    diag_ref,
    off_ref,
    low_ref,
    sol_ref,
    rows_ref,
    sems,
):
    upper_solve(
        0, [(dest_hbm, dest_ref)], inbound_ref, diag_hbm, off_hbm, low_hbm,
        diag_ref, off_ref, low_ref, sol_ref, rows_ref, sems,
    )
    store(sol_ref, answer_hbm.at[0], sems.at[5]).wait()


def whole(x):
    return x, pl.BlockSpec(memory_space=pltpu.VMEM)


def far(x):
    return x, pl.BlockSpec(memory_space=pltpu.HBM)


def anywhere(x):
    return x, pl.BlockSpec(memory_space=pl.ANY)


def call(kernel, name, operands, outs, scratch, flops, aliases={}, limit=None):
    arrays = [x for x, _ in operands]
    moved = sum(x.size * x.dtype.itemsize for x, _ in operands + outs)
    return pl.pallas_call(
        kernel,
        name=name,
        out_shape=[jax.ShapeDtypeStruct(x.shape, x.dtype) for x, _ in outs],
        in_specs=[spec for _, spec in operands],
        out_specs=[spec for _, spec in outs],
        scratch_shapes=scratch,
        input_output_aliases=aliases,
        compiler_params=pltpu.CompilerParams(vmem_limit_bytes=limit),
        cost_estimate=pl.CostEstimate(flops=flops, bytes_accessed=moved, transcendentals=0),
    )(*arrays)


def on_device(right_sides, diag_inverse, off_diagonal, target_snode, target_block):
    levels, nodes, order, lanes = right_sides.shape
    per_node = target_snode.shape[2]
    row_blocks = order // BR
    devices = lax.axis_size("snode")
    sharers = lax.axis_size("rhs")
    outgoing = nodes * per_node
    capacity = CAPACITY
    slots = devices * capacity
    local_rows = nodes * row_blocks
    couplings = levels - 1

    def diag_parts(mine):
        found = {}
        for k in shift_order(sharers)[1:]:
            step = [(y, (y + k) % sharers) for y in range(sharers)]
            found[k] = lax.ppermute(mine, "rhs", step)
        return list(found.values())

    first_parts = diag_parts(diag_inverse[0])

    block_order = lax.iota(jnp.int32, outgoing)
    flat_target = target_snode.reshape(couplings, outgoing)
    owner = flat_target // nodes
    row = flat_target % nodes * row_blocks + target_block.reshape(couplings, outgoing)
    earlier = (owner[:, :, None] == owner[:, None, :]) & (
        block_order[None, None, :] < block_order[None, :, None]
    )
    destinations = owner * capacity + jnp.sum(earlier.astype(jnp.int32), axis=2)
    slot_ids = lax.iota(jnp.int32, slots)
    placed = destinations[:, None, :] == slot_ids[None, :, None]
    sources = jnp.min(jnp.where(placed, block_order[None, None, :], outgoing), axis=2)
    ids = slot_ids.reshape(devices, 1, capacity, 1)
    placed = destinations[None, :, None, :] == ids
    sent = jnp.min(jnp.where(placed, row[None, :, None, :], local_rows), axis=3)

    def exchange(x):
        return lax.all_to_all(x, "snode", split_axis=0, concat_axis=0, tiled=True)

    vector = far(jax.ShapeDtypeStruct((nodes, order, lanes), F32))
    payload = far(jax.ShapeDtypeStruct((slots, BR, lanes), BF16))
    near_payload = whole(payload[0])
    gathered = far(jax.ShapeDtypeStruct((sharers,) + diag_inverse.shape[1:], F32))
    answer = jax.ShapeDtypeStruct(right_sides.shape, F32)
    six = pltpu.SemaphoreType.DMA((6,))
    source_smem = pltpu.SMEM((couplings, slots), jnp.int32)
    code_smem = pltpu.SMEM((couplings * capacity, devices), jnp.int32)
    dest_smem = pltpu.SMEM((couplings, outgoing), jnp.int32)
    two = pltpu.SemaphoreType.DMA((2,))
    inputs = pltpu.SemaphoreType.DMA((12,))
    vectors = pltpu.VMEM((nodes, order, lanes), F32)
    off_buffer = pltpu.VMEM(off_diagonal.shape[1:], BF16)
    diag_buffer = pltpu.VMEM(gathered[0].shape, F32)
    sums = [pltpu.VMEM((local_rows + 1, BR, lanes), F32)] * 4
    table = pltpu.VMEM((outgoing + 1, BR, lanes), BF16)
    row_table = pltpu.VMEM((local_rows + 1, BR, lanes), BF16)
    rows_scratch = pltpu.VMEM((outgoing, BR, lanes), BF16)
    blocks_buffer = pltpu.VMEM((slots, BR, lanes), BF16)
    send = [blocks_buffer, inputs, two, pltpu.SemaphoreType.DMA((8,))]
    flops = 40 * nodes * order * order * lanes
    small = 24 << 20

    def diag_operands(parts):
        return [far(diag_inverse)] + [far(x) for x in parts]

    lower, whole_diags = [None] * couplings, [None] * couplings
    lower[0], whole_diags[0], out = call(
        first_kernel,
        "first",
        [far(sources)]
        + diag_operands(first_parts)
        + [far(right_sides), far(off_diagonal)],
        [vector, gathered, payload],
        [source_smem, diag_buffer, vectors, off_buffer, vectors, table] + send,
        flops,
    )
    later_diags, out = lax.optimization_barrier((diag_inverse, out))
    later_parts = diag_parts(later_diags[1:])
    pairs_of_rows = capacity * BR // 2
    carried = sent.reshape(devices, 1, 1, couplings * capacity).astype(BF16)
    carried = jnp.pad(carried, ((0, 0), (0, 0), (0, 1), (0, lanes - couplings * capacity)))
    out = jnp.concatenate([out.reshape(devices, pairs_of_rows, 2, lanes), carried], axis=1)
    inbound = exchange(out)
    codes = inbound[:, pairs_of_rows, 0, : couplings * capacity].astype(jnp.int32).T
    inbound = inbound[:, :pairs_of_rows].reshape(slots, BR, lanes)

    for h in range(1, couplings):
        lower[h], whole_diags[h], out = call(
            functools.partial(middle_kernel, h),
            "middle",
            [far(sources), far(codes), far(inbound)]
            + diag_operands(later_parts)
            + [far(right_sides), far(off_diagonal)],
            [vector, gathered, payload],
            sums
            + [source_smem, code_smem, blocks_buffer, diag_buffer, vectors, off_buffer, vectors, table]
            + send,
            flops,
        )
        inbound = exchange(out)
    top = couplings
    answer, out = call(
        functools.partial(top_kernel, top),
        "top",
        [far(codes), far(inbound)]
        + diag_operands(later_parts)
        + [far(right_sides)],
        [far(answer), payload],
        sums + [code_smem, blocks_buffer, diag_buffer, vectors, vectors, row_table] + send,
        flops,
    )
    inbound = exchange(out)
    for h in range(couplings - 1, 0, -1):
        answer, out = call(
            functools.partial(upper_kernel, h),
            "upper",
            [far(destinations), far(codes), whole(inbound), anywhere(whole_diags[h])]
            + [anywhere(off_diagonal), anywhere(lower[h]), anywhere(answer)],
            [anywhere(answer), near_payload],
            [dest_smem, code_smem, diag_buffer, off_buffer, vectors, vectors, rows_scratch, row_table, six],
            flops,
            {6: 0},
            small,
        )
        inbound = exchange(out)
    (answer,) = call(
        last_kernel,
        "last",
        [far(destinations), whole(inbound), anywhere(whole_diags[0])]
        + [anywhere(off_diagonal), anywhere(lower[0]), anywhere(answer)],
        [anywhere(answer)],
        [dest_smem, diag_buffer, off_buffer, vectors, vectors, rows_scratch, six],
        flops,
        {5: 0},
        small,
    )
    return answer


def solution(mesh):
    in_specs = (
        P(None, "snode", None, "rhs"),
        P(None, "snode", "rhs", None),
        P(None, "snode", None, None),
        P(None, "snode", None),
        P(None, "snode", None),
    )
    out_specs = P(None, "snode", None, "rhs")
    return jax.shard_map(
        on_device, mesh=mesh, in_specs=in_specs, out_specs=out_specs, check_vma=False
    )
```
